32 devices in a mesh: gx: 4 (over y, x), gy: 4 (over z), ga: 2 (over core).
Axes of the slice: x: 2, y: 2, z: 4, core: 2. Of those that a mesh axis runs over, the one named last changes fastest.
Arguments:
- fields: float32 [5, 16, 64, 1024], P(None, 'ga', 'gx', 'gy'), may hold values from -6 to 6
- stiffness: float32 [16, 64, 1024], P('ga', 'gx', 'gy'), may hold values from 0.25 to 4
- lift_weight: float32 [5, 32], replicated, may hold values from -2.5 to 2.5
- lift_bias: float32 [32], replicated, may hold values from -3 to 3
- mix_weight: bfloat16 [32, 32], replicated, may hold values from -0.5 to 0.5
- spectral_weight: float32 [8, 32, 32, 32, 128], P('ga', 'gy', None, 'gx'), may hold values from -0.48 to 0.48
- output_bias: float32 [32], replicated, may hold values from -3 to 3
Outputs:
- layer_out: bfloat16 [16, 32, 32, 512], P('ga', None, 'gx', 'gy')
The draws below stay inside these ranges and needn't reach their ends.
All inputs are finite; a program needn't handle non-finite values.
Results may differ from the reference program's by a relative error of at most 0.01.
Values may be sent and summed in bfloat16 or wider, within the bound.
A program may use at most 128 MiB of HBM per device.

```python
import math
import jax
import jax.numpy as jnp
from jax import lax

NZ = 16
STEPS = 3
C = 32
MX = 32
MY = 64
MZ = 8
NX = 64
NY = 1024


wave_count = 48


def wave_tables(key, term_count):
    key_list = jax.random.split(key, 4)
    east_reach = max(1, min(MX // 2 - 1, NX // 16))
    north_reach = max(1, min(MY // 2 - 1, NY // 16))
    east_wave = jax.random.randint(key_list[0], (term_count,), -east_reach, east_reach + 1, dtype=jnp.int32)
    north_wave = jax.random.randint(key_list[1], (term_count,), -north_reach, north_reach + 1, dtype=jnp.int32)
    east_shift = jax.random.uniform(key_list[2], (term_count, 1), jnp.float32, 0.0, 2.0 * math.pi)
    north_shift = jax.random.uniform(key_list[3], (term_count, 1), jnp.float32, 0.0, 2.0 * math.pi)
    east_index = jnp.arange(NX, dtype=jnp.int32)
    north_index = jnp.arange(NY, dtype=jnp.int32)
    east_angle = jnp.mod(east_wave[:, None] * east_index[None, :], NX).astype(jnp.float32) * (2.0 * math.pi / NX) + east_shift
    north_angle = jnp.mod(north_wave[:, None] * north_index[None, :], NY).astype(jnp.float32) * (2.0 * math.pi / NY) + north_shift
    return (jnp.cos(east_angle), jnp.sin(east_angle), jnp.cos(north_angle), jnp.sin(north_angle))


def smooth_field(key, amplitude):
    east_cos, east_sin, north_cos, north_sin = wave_tables(key, amplitude.shape[-1])
    first = jnp.einsum('...j,jx,jy->...xy', amplitude, east_cos, north_cos)
    second = jnp.einsum('...j,jx,jy->...xy', amplitude, east_sin, north_sin)
    return first - second


def draw_fields(key, part):
    key_list = jax.random.split(key, 3)
    depth_index = jnp.arange(NZ, dtype=jnp.int32)
    orders = jnp.arange(5, dtype=jnp.int32)
    depth_angle = jnp.mod(orders[:, None] * depth_index[None, :], NZ).astype(jnp.float32) * (2.0 * math.pi / NZ)
    profile = jnp.stack([jnp.cos(depth_angle), jnp.sin(depth_angle)], axis=1)
    target = 2.5
    jagged = jax.random.normal(key_list[2], (5, NZ, NX, NY), jnp.float32)
    weights_depth = jax.random.normal(key_list[0], (5, wave_count, 5, 2), jnp.float32) * (target / math.sqrt(2.5 * wave_count))
    amplitude = jnp.einsum('fjkp,kpz->fzj', weights_depth, profile)
    smooth = smooth_field(key_list[1], amplitude)
    return jnp.clip(smooth + jagged, -6.0, 6.0)


def draw_stiffness(key, part):
    key_list = jax.random.split(key, 3)
    amplitude = jax.random.normal(key_list[0], (NZ, wave_count), jnp.float32) * (1.0 / math.sqrt(0.5 * wave_count))
    smooth = smooth_field(key_list[1], amplitude)
    jagged = jax.random.uniform(key_list[2], (NZ, NX, NY), jnp.float32, -1.0, 1.0)
    level = 0.5 + 0.3 * smooth + 0.25 * jagged
    level = jnp.clip(level, 0.0, 1.0)
    return 0.25 * jnp.exp(level * math.log(16.0))


def block_levels(rng, shape, pieces, smallest, top_value):
    factor_of, own = 1.0, jax.random.fold_in(rng, 6)
    for position, blocks in pieces:
        heights = jnp.exp(jax.random.uniform(jax.random.fold_in(own, position), (blocks,), jnp.float32, smallest / len(pieces), top_value / len(pieces)))
        factor_of = factor_of * jnp.repeat(heights, shape[position] // blocks).reshape([-1 if axis == position else 1 for axis in range(len(shape))])
    return factor_of


def gaussian(rng, dims, width, bound, cuts=(), kind=jnp.bfloat16):
    result = width * jax.random.normal(rng, dims, jnp.float32)
    if cuts:
        result = result * block_levels(rng, dims, cuts, -0.22, 0.18)
    return jnp.clip(result, -bound, bound).astype(kind)


def setup_inputs(seed: int = 0) -> dict:
    keys = jax.random.split(jax.random.key(seed), 8)
    return {
        "fields": draw_fields(jax.random.fold_in(keys[7], 71), 0),
        "stiffness": draw_stiffness(jax.random.fold_in(keys[7], 71), 0),
        "lift_weight": gaussian(keys[2], (5, C), 5 ** -0.5, 2.5, (), jnp.float32),
        "lift_bias": gaussian(keys[3], (C,), 0.5, 3.0, (), jnp.float32),
        "mix_weight": gaussian(keys[4], (C, C), (4 * C) ** -0.5, 0.5),
        "spectral_weight": gaussian(keys[5], (MZ, MX, C, C, 2 * MY), 0.08, 0.48, ((0, 2), (1, 4), (3, 4)), jnp.float32),
        "output_bias": gaussian(keys[6], (C,), 0.5, 3.0, (), jnp.float32),
    }


courant_half = 0.1
smooth_half = 0.15
mean_flow = (0.3, -0.2, 0.1)
highest = lax.Precision.HIGHEST

def step_interior(padded, stiff_part):
    center = padded[:, 1:-1, 1:-1, 1:-1]
    upper_depth = padded[:, 2:, 1:-1, 1:-1]
    lower_depth = padded[:, :-2, 1:-1, 1:-1]
    upper_east = padded[:, 1:-1, 2:, 1:-1]
    lower_east = padded[:, 1:-1, :-2, 1:-1]
    upper_north = padded[:, 1:-1, 1:-1, 2:]
    lower_north = padded[:, 1:-1, 1:-1, :-2]
    slope_depth = upper_depth - lower_depth
    slope_east = upper_east - lower_east
    slope_north = upper_north - lower_north
    curvature = upper_depth + lower_depth + upper_east + lower_east + upper_north + lower_north - 6.0 * center
    transport = mean_flow[0] * slope_east + mean_flow[1] * slope_north + mean_flow[2] * slope_depth
    diverge = slope_east[1] + slope_north[2] + slope_depth[3]
    coupling = jnp.stack([diverge, slope_east[4], slope_north[4], slope_depth[4], stiff_part * diverge])
    return center - courant_half * (transport + coupling) + smooth_half * curvature

def coarsen(fields_now):
    extent = fields_now.shape
    blocks = fields_now.reshape(extent[0], extent[1], extent[2] // 2, 2, extent[3] // 2, 2)
    return 0.25 * (blocks[:, :, :, 0, :, 0] + blocks[:, :, :, 1, :, 0] + blocks[:, :, :, 0, :, 1] + blocks[:, :, :, 1, :, 1])

def angles(frequencies, points, length):
    product = jnp.mod(frequencies[:, None] * points[None, :], length)
    return product.astype(jnp.float32) * (2.0 * math.pi / length)

def centered(number):
    return jnp.arange(number, dtype=jnp.int32) - number // 2

def forward_east_table(points, length, mode_count):
    phases = angles(centered(mode_count), points, length)
    factor = 1.0 / math.sqrt(length)
    return (jnp.stack([jnp.cos(phases).T, -jnp.sin(phases).T], axis=1) * factor).astype(jnp.bfloat16)

def forward_north_table(points, length, mode_count):
    phases = angles(centered(mode_count), points, length)
    factor = 1.0 / math.sqrt(length)
    cosines = jnp.cos(phases).T * factor
    sines = jnp.sin(phases).T * factor
    return jnp.stack([jnp.concatenate([cosines, -sines], axis=1), jnp.concatenate([sines, cosines], axis=1)], axis=0)

def inverse_north_table(points, length, mode_count):
    phases = angles(centered(mode_count), points, length)
    factor = 1.0 / math.sqrt(length)
    cosines = jnp.cos(phases) * factor
    sines = jnp.sin(phases) * factor
    return jnp.concatenate([jnp.stack([cosines, sines], axis=1), jnp.stack([-sines, cosines], axis=1)], axis=0)

def inverse_east_table(points, length, mode_count):
    phases = angles(centered(mode_count), points, length)
    factor = 1.0 / math.sqrt(length)
    return jnp.stack([jnp.cos(phases) * factor, -jnp.sin(phases) * factor], axis=1)

def forward_depth(values, points, frequencies, length):
    phases = angles(frequencies, points, length)
    factor = 1.0 / math.sqrt(length)
    cosines = jnp.cos(phases) * factor
    sines = jnp.sin(phases) * factor
    halfway = values.shape[-1] // 2
    real_in = values[..., :halfway]
    imag_in = values[..., halfway:]
    real_part = jnp.einsum('zcmn,kz->kcmn', real_in, cosines, precision=highest) + jnp.einsum('zcmn,kz->kcmn', imag_in, sines, precision=highest)
    imag_part = jnp.einsum('zcmn,kz->kcmn', imag_in, cosines, precision=highest) - jnp.einsum('zcmn,kz->kcmn', real_in, sines, precision=highest)
    return jnp.concatenate([real_part, imag_part], axis=-1)

def mix_channels(coeffs, weight):
    halfway = coeffs.shape[-1] // 2
    real_in = coeffs[..., :halfway]
    imag_in = coeffs[..., halfway:]
    weight_real = weight[..., :halfway]
    weight_imag = weight[..., halfway:]
    real_part = jnp.einsum('kcmn,kmcon->komn', real_in, weight_real, precision=highest) - jnp.einsum('kcmn,kmcon->komn', imag_in, weight_imag, precision=highest)
    imag_part = jnp.einsum('kcmn,kmcon->komn', imag_in, weight_real, precision=highest) + jnp.einsum('kcmn,kmcon->komn', real_in, weight_imag, precision=highest)
    return jnp.concatenate([real_part, imag_part], axis=-1)

def inverse_depth(values, frequencies, points, length):
    phases = angles(frequencies, points, length)
    factor = 1.0 / math.sqrt(length)
    cosines = jnp.cos(phases) * factor
    sines = jnp.sin(phases) * factor
    halfway = values.shape[-1] // 2
    real_in = values[..., :halfway]
    imag_in = values[..., halfway:]
    real_part = jnp.einsum('komn,kz->zomn', real_in, cosines, precision=highest) - jnp.einsum('komn,kz->zomn', imag_in, sines, precision=highest)
    imag_part = jnp.einsum('komn,kz->zomn', imag_in, cosines, precision=highest) + jnp.einsum('komn,kz->zomn', real_in, sines, precision=highest)
    return jnp.concatenate([real_part, imag_part], axis=-1)

def reference(fields, stiffness, lift_weight, lift_bias, mix_weight, spectral_weight, output_bias):
    fields_now = fields
    for repeat in range(STEPS):
        padded = jnp.pad(fields_now, ((0, 0), (1, 1), (1, 1), (1, 1)), mode='wrap')
        fields_now = step_interior(padded, stiffness)
    filtered = coarsen(fields_now)
    length_depth = filtered.shape[1]
    length_east = filtered.shape[2]
    length_north = filtered.shape[3]
    by_plane = jnp.transpose(filtered, (1, 0, 2, 3))

    def lift_plane(plane_fields):
        lifted_plane = jnp.einsum('fxy,fc->cxy', plane_fields, lift_weight, precision=highest) + lift_bias[:, None, None]
        return jax.nn.gelu(lifted_plane, approximate=True).astype(jnp.bfloat16)
    lifted = lax.map(lift_plane, by_plane)
    east_points = jnp.arange(length_east, dtype=jnp.int32)
    north_points = jnp.arange(length_north, dtype=jnp.int32)
    table_east = forward_east_table(east_points, length_east, MX).astype(jnp.float32)
    table_north = forward_north_table(north_points, length_north, MY)

    def plane_modes(lift_slice):
        east_modes = jnp.einsum('cxy,xpm->cpmy', lift_slice.astype(jnp.float32), table_east, precision=highest)
        return jnp.einsum('cpmy,pyq->cmq', east_modes, table_north, precision=highest)
    north_modes = lax.map(plane_modes, lifted)
    depth_points = jnp.arange(length_depth, dtype=jnp.int32)
    depth_frequencies = jnp.arange(MZ, dtype=jnp.int32)
    coeffs = forward_depth(north_modes, depth_points, depth_frequencies, length_depth)
    mixed_modes = mix_channels(coeffs, spectral_weight)
    back_depth = inverse_depth(mixed_modes, depth_frequencies, depth_points, length_depth)
    back_north_table = inverse_north_table(north_points, length_north, MY)
    back_east_table = inverse_east_table(east_points, length_east, MX)
    mix_wide = mix_weight.astype(jnp.float32)

    def plane_output(paired):
        lift_slice, modes_plane = paired
        back_north = jnp.einsum('omq,qpy->ompy', modes_plane, back_north_table, precision=highest)
        spectral = jnp.einsum('ompy,mpx->oxy', back_north, back_east_table, precision=highest).astype(jnp.bfloat16)
        direct = jnp.einsum('cxy,co->oxy', lift_slice.astype(jnp.float32), mix_wide, precision=highest)
        summed = direct + output_bias[:, None, None] + spectral.astype(jnp.float32)
        return jax.nn.gelu(summed, approximate=True).astype(jnp.bfloat16)
    return lax.map(plane_output, (lifted, back_depth))
```

```python
import math

import contextlib
import functools
import jax
import jax.numpy as jnp
import numpy as np
from jax import lax
from jax.experimental import pallas as pl
from jax.experimental.pallas import tpu as pltpu
from jax.sharding import PartitionSpec as P

STEPS = 3
MX = 32
MY = 64
MZ = 8
DEPTH_CHUNKS = 4
LIFT_CHUNKS = 4


courant_half = 0.1
smooth_half = 0.15
mean_flow = (0.3, -0.2, 0.1)
highest = lax.Precision.HIGHEST


MESH = pl.DeviceIdType.MESH
f32 = jnp.float32
bf16 = jnp.bfloat16


def gelu(v):
    return 0.5 * v * (1.0 + jnp.tanh(math.sqrt(2.0 / math.pi) * (v + 0.044715 * (v * v * v))))


def mark(name):
    return contextlib.nullcontext()


def swapped(v):
    sign = jnp.where(lax.broadcasted_iota(jnp.int32, v.shape, 1) < MY, 1.0, -1.0)
    return pltpu.roll(v, MY, 1) * sign


def dot(a, b, dims=((1,), (0,))):
    return lax.dot_general(a, b, (dims, ((), ())), preferred_element_type=f32)


def peers(axis):
    count = lax.axis_size(axis)
    me = lax.axis_index(axis)
    return me, [(d, lax.rem(me + d, count), lax.rem(me + count - d, count)) for d in range(1, count)]


def remote(src, dst, send, recv, axis, peer):
    return pltpu.make_async_remote_copy(
        src_ref=src,
        dst_ref=dst,
        send_sem=send,
        recv_sem=recv,
        device_id={axis: peer},
        device_id_type=MESH,
    )


def stencil_step(state, target, stiff, xr, yr, dims):
    NZ, NX, NY = dims
    eye = lax.broadcasted_iota(jnp.int32, (NZ * NX, NZ * NX), 0) == lax.broadcasted_iota(
        jnp.int32, (NZ * NX, NZ * NX), 1
    )
    columns = [
        [
            jnp.sum(
                jnp.where(eye, jnp.broadcast_to(yr[side, f : f + 1, :], eye.shape), 0.0),
                axis=1,
                keepdims=True,
            )
            for f in range(5)
        ]
        for side in range(2)
    ]
    row = lax.broadcasted_iota(jnp.int32, (NX, NY), 0)
    lane = lax.broadcasted_iota(jnp.int32, (NX, NY), 1)
    a, b = courant_half, smooth_half
    for z in range(NZ):
        near = []
        for f in range(5):
            c = state[f, z + 1]
            span = slice(z * NX, (z + 1) * NX)
            xl = jnp.where(row == 0, xr[0, f, z : z + 1, :].astype(f32), pltpu.roll(c, 1, 0))
            xu = jnp.where(row == NX - 1, xr[1, f, z : z + 1, :].astype(f32), pltpu.roll(c, NX - 1, 0))
            yl = jnp.where(lane == 0, columns[0][f][span], pltpu.roll(c, 1, 1))
            yu = jnp.where(lane == NY - 1, columns[1][f][span], pltpu.roll(c, NY - 1, 1))
            near.append((c, xl, xu, yl, yu, state[f, z], state[f, z + 2]))
        diverge = (
            (near[1][2] - near[1][1]) + (near[2][4] - near[2][3]) + (near[3][6] - near[3][5])
        )
        p = near[4]
        coupling = (diverge, p[2] - p[1], p[4] - p[3], p[6] - p[5], stiff[z] * diverge)
        for f in range(5):
            c, xl, xu, yl, yu, zl, zu = near[f]
            target[f, z + 1] = (
                (1.0 - 6.0 * b) * c
                + (b + a * mean_flow[0]) * xl
                + (b - a * mean_flow[0]) * xu
                + (b + a * mean_flow[1]) * yl
                + (b - a * mean_flow[1]) * yu
                + (b + a * mean_flow[2]) * zl
                + (b - a * mean_flow[2]) * zu
                - a * coupling[f]
            )


def layer_kernel(
    cfg,
    fields_hbm, stiff_hbm, ed_hbm, et_hbm, x1_hbm, x2_hbm, w_hbm, lw_hbm, lb_hbm, mix_hbm, bias_hbm,
    out,
    state, stiff, xs, xr, ys, yr, pairs, filt, ed, et, x1, x2, wv, lw, lb, mix, bias_row, wide_lift,
    lift, lift_in, both, tf, tb, p2, r2, q3, r3, c4, r4, rr, ii, mf, r5, b6, r6, r7, acc,
    local, sent, hr, r1s, r2s, r3s, r4s, r5s, r6s, r7s,
):
    G, H, A, C, CB, KB, OB, KZ, NZL, XL, YL = cfg
    Q = 2 * MY
    NX, NY = 2 * XL, 2 * YL
    gx, gx_peers = peers("gx")
    gy, gy_peers = peers("gy")
    ga = lax.axis_index("ga")
    other = lax.rem(ga + 1, A)
    barrier = pltpu.get_barrier_semaphore()
    for axis, group in (("gx", gx_peers), ("gy", gy_peers)):
        for _, peer, _ in group:
            pl.semaphore_signal(barrier, inc=1, device_id={axis: peer}, device_id_type=MESH)
    pl.semaphore_signal(barrier, inc=1, device_id={"ga": other}, device_id_type=MESH)
    loads = [
        pltpu.make_async_copy(source, target, local.at[n])
        for n, (source, target) in enumerate(
            (
                (fields_hbm, state.at[0, :, pl.ds(1, NZL)]),
                (stiff_hbm, stiff),
                (ed_hbm.at[gy], ed),
                (et_hbm.at[gy], et),
                (x1_hbm, x1),
                (x2_hbm, x2),
                (w_hbm, wv),
                (lw_hbm, lw),
                (lb_hbm, lb),
                (mix_hbm, mix),
                (bias_hbm, bias_row),
            )
        )
    ]
    loads[0].start()

    HALF = KZ // 2
    NZC = DEPTH_CHUNKS
    ZC = NZL // NZC
    NZ = NZL * A
    slots = list(range(0, KZ, 2)) + list(range(1, KZ, 2))

    def own(values):
        picked = jnp.float32(values[0])
        for n in range(1, A):
            picked = jnp.where(ga == n, jnp.float32(values[n]), picked)
        return picked

    def angles(z, owner, k):
        v = [
            2.0 * math.pi * ((((n + owner) % A * KZ + k) * (n * NZL + z)) % NZ) / NZ for n in range(A)
        ]
        return own([math.cos(x) for x in v]), own([math.sin(x) for x in v])

    def build_table():
        loads[2].wait()
        loads[3].wait()
        for z in range(NZL):
            for owner in range(A):
                for j, k in enumerate(slots):
                    cos, sin = angles(z, owner, k)
                    span = slice((j % HALF) * Q, (j % HALF + 1) * Q)
                    if owner == 0:
                        block = ed[0] * cos + ed[1] * sin
                        tf[j // HALF, z * YL : (z + 1) * YL, span] = block.astype(bf16)
                    block = et[0] * cos + et[1] * sin
                    tb[2 * owner + j // HALF, span, z * YL : (z + 1) * YL] = block.astype(bf16)

    spread = jnp.where(
        lax.broadcasted_iota(jnp.int32, (C * XL, C), 0) // XL
        == lax.broadcasted_iota(jnp.int32, (C * XL, C), 1),
        1.0,
        0.0,
    )

    def tall(values):
        return jnp.sum(spread * values, axis=1, keepdims=True)

    def build_lift():
        for n in (7, 8):
            loads[n].wait()
        for f in range(6):
            values = lw[f : f + 1, :] if f < 5 else lb[...]
            wide_lift[f] = jnp.broadcast_to(tall(values), (C * XL, YL))

    with mark("ld0"):
        loads[0].wait()
    eye = lax.broadcasted_iota(jnp.int32, (NZL * NX, NZL * NX), 0) == lax.broadcasted_iota(
        jnp.int32, (NZL * NX, NZL * NX), 1
    )
    for t in range(STEPS):
        now = state.at[t]
        with mark("pack%d" % t):
            for side, (edge_x, edge_y) in enumerate(((NX - 1, NY - 1), (0, 0))):
                for f in range(5):
                    for z in range(NZL):
                        row = now[f, z + 1, edge_x : edge_x + 1, :]
                        xs[t, side, f, z : z + 1, :] = row.astype(bf16)
                    column = now[f, 1 : NZL + 1, :, edge_y : edge_y + 1].reshape(NZL * NX, 1)
                    ys[t, side, f : f + 1, :] = jnp.sum(
                        jnp.where(eye, jnp.broadcast_to(column, eye.shape), 0.0),
                        axis=0,
                        keepdims=True,
                    )
        if t == 0:
            with mark("barrier"):
                pl.semaphore_wait(barrier, (G - 1) + (H - 1) + 1)
        for side in range(2):
            shift = 1 if side == 0 else -1
            tx, ty, ta = (
                lax.rem(lax.axis_index(n) + lax.axis_size(n) + shift, lax.axis_size(n))
                for n in ("gx", "gy", "ga")
            )
            plane, halo = (NZL, 0) if side == 0 else (1, NZL + 1)
            remote(ys.at[t, side], yr.at[t, side], sent.at[0], hr.at[t, 0], "gy", ty).start()
            remote(xs.at[t, side], xr.at[t, side], sent.at[1], hr.at[t, 1], "gx", tx).start()
            remote(now.at[:, plane], now.at[:, halo], sent.at[2], hr.at[t, 2], "ga", ta).start()
        if t == 0:
            for load in loads[1:]:
                load.start()
            with mark("table"):
                build_table()
                loads[1].wait()
        if t == STEPS - 1:
            with mark("buildlift"):
                build_lift()
        with mark("halo%d" % t):
            remote(ys.at[t], yr.at[t], sent.at[0], hr.at[t, 0], "gy", gy).wait_recv()
            remote(xs.at[t], xr.at[t], sent.at[1], hr.at[t, 1], "gx", gx).wait_recv()
            two = now.at[:, pl.ds(0, 2)]
            remote(two, two, sent.at[2], hr.at[t, 2], "ga", other).wait_recv()
        with mark("stencil%d" % t):
            stencil_step(now, state.at[t + 1], stiff, xr.at[t], yr.at[t], (NZL, NX, NY))

    with mark("filter"):
        twin = lax.broadcasted_iota(jnp.int32, (NY, YL), 0) // 2 == lax.broadcasted_iota(
            jnp.int32, (NY, YL), 1
        )
        twin = jnp.where(twin, 1.0, 0.0)
        for f in range(5):
            pairs[f] = lax.dot_general(
                state[STEPS, f, 1 : NZL + 1].reshape(NZL * NX, NY),
                twin,
                (((1,), (0,)), ((), ())),
                precision=highest,
                preferred_element_type=f32,
            )
            for z in range(NZL):
                filt[f, z] = 0.25 * (
                    pairs[f, pl.ds(z * NX, XL, stride=2), :]
                    + pairs[f, pl.ds(z * NX + 1, XL, stride=2), :]
                )

    def lift_two(pair, carry):
        rows = pl.ds(pl.multiple_of(pair * 2 * XL, 2 * XL), 2 * XL)
        weights = [wide_lift[f, rows, :] for f in range(6)]
        for z in range(NZL):
            v = weights[5]
            for f in range(5):
                v = v + jnp.concatenate([filt[f, z], filt[f, z]], axis=0) * weights[f]
            lift[rows, z * YL : (z + 1) * YL] = gelu(v).astype(bf16)
        return carry

    LC = LIFT_CHUNKS
    RC = C * XL // LC
    with mark("lift"):
        for n in range(LC):
            lax.fori_loop(n * C // 2 // LC, (n + 1) * C // 2 // LC, lift_two, 0)
            rows = pl.ds(n * RC, RC)
            remote(lift.at[rows], lift_in.at[rows], sent.at[3], r1s.at[n], "ga", other).start()
    for n in range(LC):
        rows = pl.ds(n * RC, RC)
        with mark("w1"):
            remote(lift.at[rows], lift_in.at[rows], sent.at[3], r1s.at[n], "ga", other).wait_recv()
        with mark("sumdiff"):
            mine, theirs = lift[rows], lift_in[rows]
            both[0, rows] = mine + theirs
            both[1, rows] = mine - theirs

    for parity in range(2):
        with mark("dot1"):
            modes = dot(both[parity], tf[parity]).astype(bf16)
            for i in range(HALF):
                h = parity * HALF + i
                p2[h] = modes[:, i * Q : (i + 1) * Q].reshape(p2.shape[1:])
        for i in range(HALF):
            h = parity * HALF + i
            for _, peer, _ in gx_peers:
                remote(p2.at[h, peer], r2.at[h, gx], sent.at[4], r2s.at[h], "gx", peer).start()
            r2[h, gx] = p2[h, gx]

    with mark("direct"):
        loads[9].wait()
        loads[10].wait()
        bias = tall(bias_row[...])
        wide = dot(spread.astype(bf16), mix[...], ((1,), (1,))).astype(bf16)
        wide = dot(wide, spread.astype(bf16), ((1,), (1,)))
        same = lax.rem(lax.broadcasted_iota(jnp.int32, wide.shape, 0), XL) == lax.rem(
            lax.broadcasted_iota(jnp.int32, wide.shape, 1), XL
        )
        mixk = jnp.where(same, wide, 0.0).astype(bf16)
        for j in range(NZC):
            span = slice(j * ZC * YL, (j + 1) * ZC * YL)
            acc[:, span] = dot(mixk, lift[:, span]) + bias
        loads[4].wait()
        loads[5].wait()
        loads[6].wait()

    def turn(x, v):
        both_parts = dot(x[...], v)
        rows = both_parts.shape[0] // 2
        return (both_parts[:rows] + swapped(both_parts[rows:])).astype(bf16)

    def step_x(h):
        part = r2.at[h, pl.ds(0, G - 1)]
        with mark("w2"):
            remote(part, part, sent.at[4], r2s.at[h], "gx", gx).wait_recv()
        with mark("xdot"):
            q3[h] = turn(x1, r2[h].reshape(C * XL, Q)).reshape(q3.shape[1:])
        for n, peer, _ in gy_peers:
            remote(q3.at[h, peer], r3.at[h, n - 1], sent.at[5], r3s.at[h], "gy", peer).start()

    def step_y(h):
        with mark("w3"):
            remote(r3.at[h], r3.at[h], sent.at[5], r3s.at[h], "gy", gy).wait_recv()
        total = q3[h, gy].astype(f32)
        for n in range(H - 1):
            total = total + r3[h, n].astype(f32)
        c4[h] = total.astype(bf16)
        for _, peer, _ in gx_peers:
            remote(c4.at[h], r4.at[h, gx], sent.at[6], r4s.at[h], "gx", peer).start()
        r4[h, gx] = c4[h]

    low = lax.broadcasted_iota(jnp.int32, (C * KB, Q), 1) < MY

    def step_mix(h):
        part = r4.at[h, pl.ds(0, G - 1)]
        with mark("w4"):
            remote(part, part, sent.at[6], r4s.at[h], "gx", gx).wait_recv()
        with mark("mix"):
            v = r4[h].reshape(C * KB, Q).astype(f32)
            turned = pltpu.roll(v, MY, 1)
            rr[h] = jnp.where(low, v, turned)
            ii[h] = jnp.where(low, turned, v)

            def mix_one(kx, carry):
                a = [None] * 4
                b = [None] * 4
                for c in range(C):
                    w = wv[slots[h], kx, c]
                    x = w * rr[h, pl.ds(c * KB + kx, 1), :]
                    y = w * ii[h, pl.ds(c * KB + kx, 1), :]
                    n = c % 4
                    a[n] = x if a[n] is None else a[n] + x
                    b[n] = y if b[n] is None else b[n] + y
                mf[h, kx] = ((a[0] + a[1]) + (a[2] + a[3])) - swapped((b[0] + b[1]) + (b[2] + b[3]))
                return carry

            lax.fori_loop(0, KB, mix_one, 0)
            r5[h, gy] = mf[h].reshape(KB * OB, Q).astype(bf16)
        for _, peer, _ in gy_peers:
            remote(r5.at[h, gy], r5.at[h, gy], sent.at[7], r5s.at[h], "gy", peer).start()

    def step_back(h):
        part = r5.at[h, pl.ds(0, H - 1)]
        with mark("w5"):
            remote(part, part, sent.at[7], r5s.at[h], "gy", gy).wait_recv()
        with mark("back"):
            b6[h] = turn(x2, r5[h].reshape(H * KB * OB, Q)).reshape(b6.shape[1:])
        for _, peer, _ in gx_peers:
            remote(b6.at[h, peer], r6.at[h, gx], sent.at[8], r6s.at[h], "gx", peer).start()
        r6[h, gx] = b6[h, gx]

    def step_pass(h):
        part = r6.at[h, pl.ds(0, G - 1)]
        with mark("w6"):
            remote(part, part, sent.at[8], r6s.at[h], "gx", gx).wait_recv()
        remote(r6.at[h], r7.at[h], sent.at[9], r7s.at[h], "ga", other).start()

    def modes_of(ref, parity):
        parts = [ref[parity * HALF + i].reshape(C * XL, Q) for i in range(HALF)]
        return jnp.concatenate(parts, axis=1)

    def gather(ref, owner, parity):
        with mark("zdot"):
            y = modes_of(ref, parity)
            for j in range(NZC):
                span = slice(j * ZC * YL, (j + 1) * ZC * YL)
                acc[:, span] = acc[:, span] + dot(y, tb[2 * owner + parity, :, span])

    def arrived(h):
        with mark("w7"):
            remote(r6.at[h], r7.at[h], sent.at[9], r7s.at[h], "ga", other).wait_recv()

    for h in range(KZ):
        step_x(h)
    for h in range(KZ - 1):
        step_y(h)
    step_mix(0)
    step_y(KZ - 1)
    for h in range(1, KZ):
        step_mix(h)
    for h in range(KZ - 1):
        step_back(h)
    step_pass(0)
    step_back(KZ - 1)
    for h in range(1, HALF):
        step_pass(h)
    gather(r6, 0, 0)
    for h in range(HALF, KZ):
        step_pass(h)
    gather(r6, 0, 1)
    for h in range(HALF):
        arrived(h)
    gather(r7, 1, 0)
    for h in range(HALF, KZ):
        arrived(h)
    with mark("final"):
        last = modes_of(r7, 1)
        for j in range(NZC):
            span = slice(j * ZC * YL, (j + 1) * ZC * YL)
            done = gelu(acc[:, span] + dot(last, tb[3, :, span])).astype(bf16)
            for z in range(ZC):
                out[j * ZC + z] = done[:, z * YL : (z + 1) * YL].reshape(C, XL, YL)

    two = state.at[pl.ds(0, STEPS), :, pl.ds(0, 2)]
    for n, (axis, ref) in enumerate(
        (
            ("gy", ys),
            ("gx", xs),
            ("ga", two),
            ("ga", lift),
            ("gx", p2.at[:, pl.ds(0, G - 1)]),
            ("gy", q3.at[:, pl.ds(0, H - 1)]),
            ("gx", r4.at[:, pl.ds(0, G - 1)]),
            ("gy", r5.at[:, pl.ds(0, H - 1)]),
            ("gx", b6.at[:, pl.ds(0, G - 1)]),
            ("ga", r6),
        )
    ):
        remote(ref, ref, sent.at[n], sent.at[n], axis, lax.axis_index(axis)).wait_send()


def east_tables(G, H, XL, C):
    CB, KB, OB = C // G, MX // H, C // G
    length = G * XL
    k = np.arange(MX) - MX // 2
    ang = 2.0 * np.pi * ((k[:, None] * np.arange(length)[None, :]) % length) / length
    scale = 1.0 / math.sqrt(length)
    cos, sin = np.cos(ang) * scale, np.sin(ang) * scale
    cos[np.abs(cos) < 1e-12] = 0.0
    sin[np.abs(sin) < 1e-12] = 0.0

    def forward(t):
        t = t.reshape(H, KB, G, XL)
        full = np.einsum("hkgx,cd->hckgdx", t, np.eye(CB))
        return full.reshape(H * CB * KB, G * CB * XL)

    def inverse(t):
        t = t.reshape(H, KB, G, XL)
        full = np.einsum("hkgx,op->goxhkp", t, np.eye(OB))
        return full.reshape(G * OB * XL, H * KB * OB)

    x1 = np.concatenate([forward(cos), forward(sin)], axis=0)
    x2 = np.concatenate([inverse(cos), -inverse(sin)], axis=0)
    return jnp.asarray(x1, bf16), jnp.asarray(x2, bf16)


def north_tables(H, YL, NZ):
    length = H * YL
    n = np.arange(MY) - MY // 2
    u = 2.0 * np.pi * ((np.arange(length)[:, None] * n[None, :]) % length) / length
    scale = 1.0 / math.sqrt(length * NZ)
    cu, su = np.cos(u) * scale, np.sin(u) * scale
    both = np.stack([np.concatenate([cu, -su], axis=1), np.concatenate([-su, -cu], axis=1)])
    both = both.reshape(2, H, YL, 2 * MY)
    return jnp.asarray(both.transpose(1, 0, 2, 3), f32), jnp.asarray(both.transpose(1, 0, 3, 2), f32)


def shards(fields, stiffness, lift_weight, lift_bias, mix_weight, spectral_weight, output_bias):
    G, H, A = (lax.axis_size(n) for n in ("gx", "gy", "ga"))
    _, NZL, NX, NY = fields.shape
    XL, YL = NX // 2, NY // 2
    C = lift_weight.shape[1]
    CB, KB, OB, KZ, Q = C // G, MX // H, C // G, MZ // A, 2 * MY
    NZ = NZL * A
    x1, x2 = east_tables(G, H, XL, C)
    ed, et = north_tables(H, YL, NZ)
    cfg = (G, H, A, C, CB, KB, OB, KZ, NZL, XL, YL)
    vmem_bytes = 67043328 - 2 * NZL * C * XL * YL
    hbm = pl.BlockSpec(memory_space=pltpu.HBM)
    LC, HALF = LIFT_CHUNKS, KZ // 2
    dma = pltpu.SemaphoreType.DMA
    V = pltpu.VMEM
    return pl.pallas_call(
        functools.partial(layer_kernel, cfg),
        out_shape=V((NZL, C, XL, YL), bf16),
        in_specs=[hbm] * 11,
        out_specs=pl.BlockSpec(memory_space=V),
        scratch_shapes=[
            V((STEPS + 1, 5, NZL + 2, NX, NY), f32),
            V((NZL, NX, NY), f32),
            V((STEPS, 2, 5, NZL, NY), bf16),
            V((STEPS, 2, 5, NZL, NY), bf16),
            V((STEPS, 2, 5, NZL * NX), f32),
            V((STEPS, 2, 5, NZL * NX), f32),
            V((5, NZL * NX, YL), f32),
            V((5, NZL, XL, YL), f32),
            V(ed.shape[1:], f32),
            V(et.shape[1:], f32),
            V(x1.shape, bf16),
            V(x2.shape, bf16),
            V(spectral_weight.shape, f32),
            V(lift_weight.shape, f32),
            V((1, C), f32),
            V(mix_weight.shape, bf16),
            V((1, C), f32),
            V((6, C * XL, YL), f32),
            V((C * XL, NZL * YL), bf16),
            V((C * XL, NZL * YL), bf16),
            V((2, C * XL, NZL * YL), bf16),
            V((2, NZL * YL, HALF * Q), bf16),
            V((2 * A, HALF * Q, NZL * YL), bf16),
            V((KZ, G, CB * XL, Q), bf16),
            V((KZ, G, CB * XL, Q), bf16),
            V((KZ, H, CB * KB, Q), bf16),
            V((KZ, H - 1, CB * KB, Q), bf16),
            V((KZ, CB * KB, Q), bf16),
            V((KZ, G, CB * KB, Q), bf16),
            V((KZ, C * KB, Q), f32),
            V((KZ, C * KB, Q), f32),
            V((KZ, KB, OB, Q), f32),
            V((KZ, H, KB * OB, Q), bf16),
            V((KZ, G, OB * XL, Q), bf16),
            V((KZ, G, OB * XL, Q), bf16),
            V((KZ, G, OB * XL, Q), bf16),
            V((C * XL, NZL * YL), f32),
            dma((11,)), dma((10,)), dma((STEPS, 3)),
            dma((LC,)), dma((KZ,)), dma((KZ,)), dma((KZ,)), dma((KZ,)), dma((KZ,)), dma((KZ,)),
        ],
        compiler_params=pltpu.CompilerParams(collective_id=0, has_side_effects=True, vmem_limit_bytes=vmem_bytes),
    )(
        fields, stiffness, ed, et, x1, x2, spectral_weight,
        lift_weight, lift_bias[None, :], mix_weight, output_bias[None, :],
    )


def solution(mesh):
    placed = (
        P(None, "ga", "gx", "gy"),
        P("ga", "gx", "gy"),
        P(),
        P(),
        P(),
        P("ga", "gy", None, "gx", None),
        P(),
    )
    return jax.shard_map(
        shards, mesh=mesh, in_specs=placed, out_specs=P("ga", None, "gx", "gy"), check_vma=False
    )
```

```python
import math

import contextlib
import functools
import jax
import jax.numpy as jnp
import numpy as np
from jax import lax
from jax.experimental import pallas as pl
from jax.experimental.pallas import tpu as pltpu
from jax.sharding import PartitionSpec as P

STEPS = 3
MX = 32
MY = 64
MZ = 8
DEPTH_CHUNKS = 4


courant_half = 0.1
smooth_half = 0.15
mean_flow = (0.3, -0.2, 0.1)
highest = lax.Precision.HIGHEST


MESH = pl.DeviceIdType.MESH
f32 = jnp.float32
bf16 = jnp.bfloat16


def gelu(v):
    scale = math.sqrt(2.0 / math.pi)
    half = 0.5 * v
    return half + half * jnp.tanh(v * (scale + (0.044715 * scale) * (v * v)))


def mark(name):
    return contextlib.nullcontext()


def swapped(v):
    sign = jnp.where(lax.broadcasted_iota(jnp.int32, v.shape, 1) < MY, 1.0, -1.0)
    return pltpu.roll(v, MY, 1) * sign


def dot(a, b, dims=((1,), (0,))):
    return lax.dot_general(a, b, (dims, ((), ())), preferred_element_type=f32)


def peers(axis):
    count = lax.axis_size(axis)
    me = lax.axis_index(axis)
    return me, [(d, lax.rem(me + d, count), lax.rem(me + count - d, count)) for d in range(1, count)]


def remote(src, dst, send, recv, axis, peer):
    return pltpu.make_async_remote_copy(
        src_ref=src,
        dst_ref=dst,
        send_sem=send,
        recv_sem=recv,
        device_id={axis: peer},
        device_id_type=MESH,
    )


def stencil_step(state, target, stiff, xr, yr, dims):
    NZ, NX, NY = dims
    eye = lax.broadcasted_iota(jnp.int32, (NZ * NX, NZ * NX), 0) == lax.broadcasted_iota(
        jnp.int32, (NZ * NX, NZ * NX), 1
    )
    columns = [
        [
            jnp.sum(
                jnp.where(eye, jnp.broadcast_to(yr[side, f : f + 1, :], eye.shape), 0.0),
                axis=1,
                keepdims=True,
            )
            for f in range(5)
        ]
        for side in range(2)
    ]
    row = lax.broadcasted_iota(jnp.int32, (NX, NY), 0)
    lane = lax.broadcasted_iota(jnp.int32, (NX, NY), 1)
    a, b = courant_half, smooth_half
    for z in range(NZ):
        near = []
        for f in range(5):
            c = state[f, z + 1]
            span = slice(z * NX, (z + 1) * NX)
            xl = jnp.where(row == 0, xr[0, f, z : z + 1, :].astype(f32), pltpu.roll(c, 1, 0))
            xu = jnp.where(row == NX - 1, xr[1, f, z : z + 1, :].astype(f32), pltpu.roll(c, NX - 1, 0))
            yl = jnp.where(lane == 0, columns[0][f][span], pltpu.roll(c, 1, 1))
            yu = jnp.where(lane == NY - 1, columns[1][f][span], pltpu.roll(c, NY - 1, 1))
            near.append((c, xl, xu, yl, yu, state[f, z], state[f, z + 2]))
        diverge = (
            (near[1][2] - near[1][1]) + (near[2][4] - near[2][3]) + (near[3][6] - near[3][5])
        )
        p = near[4]
        coupling = (diverge, p[2] - p[1], p[4] - p[3], p[6] - p[5], stiff[z] * diverge)
        for f in range(5):
            c, xl, xu, yl, yu, zl, zu = near[f]
            target[f, z + 1] = (
                (1.0 - 6.0 * b) * c
                + (b + a * mean_flow[0]) * xl
                + (b - a * mean_flow[0]) * xu
                + (b + a * mean_flow[1]) * yl
                + (b - a * mean_flow[1]) * yu
                + (b + a * mean_flow[2]) * zl
                + (b - a * mean_flow[2]) * zu
                - a * coupling[f]
            )


def layer_kernel(
    cfg,
    fields_hbm, stiff_hbm, ed_hbm, et_hbm, x1_hbm, x2_hbm, w_hbm, lw_hbm, lb_hbm, mix_hbm, bias_hbm,
    out,
    state, stiff, xs, xr, ys, yr, pairs, filt, ed, et, x1, x2, wv, lw, lb, mix, bias_row, wide_lift,
    spread_in, lift, lift_in, both, tf, tb, p2, r2, q3, r3, c4, r4, rr, ii, mf, r5, b6, r6, r7, acc,
    local, sent, hr, r1s, r2s, r3s, r4s, r5s, r6s, r7s,
):
    G, H, A, C, CB, KB, OB, KZ, NZL, XL, YL = cfg
    Q = 2 * MY
    NX, NY = 2 * XL, 2 * YL
    gx, gx_peers = peers("gx")
    gy, gy_peers = peers("gy")
    ga = lax.axis_index("ga")
    other = lax.rem(ga + 1, A)
    barrier = pltpu.get_barrier_semaphore()
    for axis, group in (("gx", gx_peers), ("gy", gy_peers)):
        for _, peer, _ in group:
            pl.semaphore_signal(barrier, inc=1, device_id={axis: peer}, device_id_type=MESH)
    pl.semaphore_signal(barrier, inc=1, device_id={"ga": other}, device_id_type=MESH)
    loads = [
        pltpu.make_async_copy(source, target, local.at[n])
        for n, (source, target) in enumerate(
            (
                *((fields_hbm.at[f], state.at[0, f, pl.ds(1, NZL)]) for f in range(5)),
                (stiff_hbm, stiff),
                (ed_hbm.at[gy], ed),
                (et_hbm.at[gy], et),
                (x1_hbm, x1),
                (x2_hbm, x2),
                (w_hbm, wv),
                (lw_hbm, lw),
                (lb_hbm, lb),
                (mix_hbm, mix),
                (bias_hbm, bias_row),
            )
        )
    ]
    first, loads = loads[:5], loads[5:]
    for load in first:
        load.start()

    HALF = KZ // 2
    NZC = DEPTH_CHUNKS
    ZC = NZL // NZC
    NZ = NZL * A
    slots = list(range(0, KZ, 2)) + list(range(1, KZ, 2))

    def own(values):
        picked = jnp.float32(values[0])
        for n in range(1, A):
            picked = jnp.where(ga == n, jnp.float32(values[n]), picked)
        return picked

    def angles(z, owner, k):
        v = [
            2.0 * math.pi * ((((n + owner) % A * KZ + k) * (n * NZL + z)) % NZ) / NZ for n in range(A)
        ]
        return own([math.cos(x) for x in v]), own([math.sin(x) for x in v])

    def build_table():
        loads[1].wait()
        loads[2].wait()
        for z in range(NZL):
            for owner in range(A):
                for j, k in enumerate(slots):
                    cos, sin = angles(z, owner, k)
                    span = slice((j % HALF) * Q, (j % HALF + 1) * Q)
                    if owner == 0:
                        block = ed[0] * cos + ed[1] * sin
                        rows = slice(z % ZC * YL, (z % ZC + 1) * YL)
                        tf[j // HALF, z // ZC, rows, span] = block.astype(bf16)
                    block = et[0] * cos + et[1] * sin
                    tb[2 * owner + j // HALF, span, z * YL : (z + 1) * YL] = block.astype(bf16)

    spread = jnp.where(
        lax.broadcasted_iota(jnp.int32, (C * XL, C), 0) // XL
        == lax.broadcasted_iota(jnp.int32, (C * XL, C), 1),
        1.0,
        0.0,
    )

    def tall(values):
        return jnp.sum(spread * values, axis=1, keepdims=True)

    def build_lift():
        for n in (6, 7):
            loads[n].wait()
        row = lax.broadcasted_iota(jnp.int32, (C * XL, 16 * XL), 0)
        lane = lax.broadcasted_iota(jnp.int32, (C * XL, 16 * XL), 1)
        group = lane // XL
        table = jnp.zeros((C * XL, 16 * XL), f32)
        for f in range(6):
            values = tall(lw[f : f + 1, :] if f < 5 else lb[...])
            high = values.astype(bf16).astype(f32)
            rest = values - high
            if f < 5:
                table = jnp.where((group == f) | (group == 5 + f), high, table)
                table = jnp.where(group == 10 + f, rest, table)
        same = lax.rem(row, XL) == lax.rem(lane, XL)
        table = jnp.where(same & (group < 15), table, 0.0)
        table = jnp.where(lane == 15 * XL, high, table)
        table = jnp.where(lane == 15 * XL + 1, rest, table)
        wide_lift[...] = table.astype(bf16)

    with mark("ld0"):
        for load in first:
            load.wait()
    eye = lax.broadcasted_iota(jnp.int32, (NZL * NX, NZL * NX), 0) == lax.broadcasted_iota(
        jnp.int32, (NZL * NX, NZL * NX), 1
    )
    for t in range(STEPS):
        now = state.at[t]
        with mark("pack%d" % t):
            for side, (edge_x, edge_y) in enumerate(((NX - 1, NY - 1), (0, 0))):
                for f in range(5):
                    for z in range(NZL):
                        row = now[f, z + 1, edge_x : edge_x + 1, :]
                        xs[t, side, f, z : z + 1, :] = row.astype(bf16)
                    column = now[f, 1 : NZL + 1, :, edge_y : edge_y + 1].reshape(NZL * NX, 1)
                    ys[t, side, f : f + 1, :] = jnp.sum(
                        jnp.where(eye, jnp.broadcast_to(column, eye.shape), 0.0),
                        axis=0,
                        keepdims=True,
                    )
        if t == 0:
            with mark("barrier"):
                pl.semaphore_wait(barrier, (G - 1) + (H - 1) + 1)
        for side in range(2):
            shift = 1 if side == 0 else -1
            tx, ty, ta = (
                lax.rem(lax.axis_index(n) + lax.axis_size(n) + shift, lax.axis_size(n))
                for n in ("gx", "gy", "ga")
            )
            plane, halo = (NZL, 0) if side == 0 else (1, NZL + 1)
            remote(ys.at[t, side], yr.at[t, side], sent.at[0], hr.at[t, 0], "gy", ty).start()
            remote(xs.at[t, side], xr.at[t, side], sent.at[1], hr.at[t, 1], "gx", tx).start()
            remote(now.at[:, plane], now.at[:, halo], sent.at[2], hr.at[t, 2], "ga", ta).start()
        if t == 0:
            for load in loads:
                load.start()
            with mark("table"):
                build_table()
                loads[0].wait()
        if t == STEPS - 1:
            with mark("buildlift"):
                build_lift()
        with mark("halo%d" % t):
            remote(ys.at[t], yr.at[t], sent.at[0], hr.at[t, 0], "gy", gy).wait_recv()
            remote(xs.at[t], xr.at[t], sent.at[1], hr.at[t, 1], "gx", gx).wait_recv()
            two = now.at[:, pl.ds(0, 2)]
            remote(two, two, sent.at[2], hr.at[t, 2], "ga", other).wait_recv()
        with mark("stencil%d" % t):
            stencil_step(now, state.at[t + 1], stiff, xr.at[t], yr.at[t], (NZL, NX, NY))

    with mark("filter"):
        twin = lax.rem(lax.broadcasted_iota(jnp.int32, (2 * NY, YL), 0), NY) // 2
        twin = jnp.where(twin == lax.broadcasted_iota(jnp.int32, (2 * NY, YL), 1), 0.25, 0.0)
        for f in range(5):
            v = state[STEPS, f, 1 : NZL + 1].reshape(NZL * NX, NY)
            high = v.astype(bf16)
            rows = pl.ds(f * NZL * NX, NZL * NX)
            pairs[rows, :NY] = high
            pairs[rows, NY:] = (v - high.astype(f32)).astype(bf16)
        for rows in (pl.ds(0, 5 * NZL * XL), pl.ds(5 * NZL * XL, 5 * NZL * XL)):
            filt[rows] = dot(pairs[rows], twin.astype(bf16))

        def mean(f, z):
            start = (f * NZL + z) * NX
            return filt[pl.ds(start, XL, stride=2), :] + filt[pl.ds(start + 1, XL, stride=2), :]

        for z in range(NZL):
            v = jnp.concatenate([mean(f, z) for f in range(5)], axis=0)
            high = v.astype(bf16).astype(f32)
            v = jnp.concatenate([high, v - high, high, jnp.ones((XL, YL), f32)], axis=0)
            span = slice(z % ZC * YL, (z % ZC + 1) * YL)
            spread_in[z // ZC, :, span] = v.astype(bf16)

    with mark("lift"):
        for n in range(0, NZC, 2):
            for i in range(n, n + 2):
                lift[i] = gelu(dot(wide_lift[...], spread_in[i])).astype(bf16)
            for i in range(n, n + 2):
                remote(lift.at[i], lift_in.at[i], sent.at[3], r1s.at[i], "ga", other).start()
    for n in range(NZC):
        with mark("w1"):
            remote(lift.at[n], lift_in.at[n], sent.at[3], r1s.at[n], "ga", other).wait_recv()
        with mark("sumdiff"):
            mine, theirs = lift[n], lift_in[n]
            both[0, n] = mine + theirs
            both[1, n] = mine - theirs

    with mark("dot1"):
        for parity in range(2):
            modes = dot(both[parity, 0], tf[parity, 0])
            for n in range(1, NZC):
                modes = modes + dot(both[parity, n], tf[parity, n])
            modes = modes.astype(bf16)
            for i in range(HALF):
                p2[parity * HALF + i] = modes[:, i * Q : (i + 1) * Q].reshape(p2.shape[1:])
    for h in range(KZ):
        for _, peer, _ in gx_peers:
            remote(p2.at[h, peer], r2.at[h, gx], sent.at[4], r2s.at[h], "gx", peer).start()
    for h in range(KZ):
        r2[h, gx] = p2[h, gx]

    with mark("direct"):
        loads[8].wait()
        loads[9].wait()
        bias = tall(bias_row[...])
        wide = dot(spread.astype(bf16), mix[...], ((1,), (1,))).astype(bf16)
        wide = dot(wide, spread.astype(bf16), ((1,), (1,)))
        same = lax.rem(lax.broadcasted_iota(jnp.int32, wide.shape, 0), XL) == lax.rem(
            lax.broadcasted_iota(jnp.int32, wide.shape, 1), XL
        )
        mixk = jnp.where(same, wide, 0.0).astype(bf16)
        for j in range(NZC):
            span = slice(j * ZC * YL, (j + 1) * ZC * YL)
            acc[:, span] = dot(mixk, lift[j]) + bias
        loads[3].wait()
        loads[4].wait()
        loads[5].wait()

    def turn(x, v):
        rows = x.shape[0] // 2
        return (dot(x[:rows], v) + swapped(dot(x[rows:], v))).astype(bf16)

    def staggered(h, send):
        @pl.when(ga == 0)
        def _():
            send(h)

        if h == KZ - 1:

            @pl.when(ga != 0)
            def _():
                for i in range(KZ):
                    send(i)

    def step_x(h):
        part = r2.at[h, pl.ds(0, G - 1)]
        with mark("w2"):
            remote(part, part, sent.at[4], r2s.at[h], "gx", gx).wait_recv()
        with mark("xdot"):
            q3[h] = turn(x1, r2[h].reshape(C * XL, Q)).reshape(q3.shape[1:])
        staggered(h, send_x)

    def send_x(h):
        for n, peer, _ in gy_peers:
            remote(q3.at[h, peer], r3.at[h, n - 1], sent.at[5], r3s.at[h], "gy", peer).start()

    def step_y(h):
        with mark("w3"):
            remote(r3.at[h], r3.at[h], sent.at[5], r3s.at[h], "gy", gy).wait_recv()
        total = q3[h, gy].astype(f32)
        for n in range(H - 1):
            total = total + r3[h, n].astype(f32)
        c4[h] = total.astype(bf16)
        for _, peer, _ in gx_peers:
            remote(c4.at[h], r4.at[h, gx], sent.at[6], r4s.at[h], "gx", peer).start()
        r4[h, gx] = c4[h]

    low = lax.broadcasted_iota(jnp.int32, (CB * KB, Q), 1) < MY

    def step_mix(h):
        part = r4.at[h, pl.ds(0, G - 1)]
        with mark("w4"):
            remote(part, part, sent.at[6], r4s.at[h], "gx", gx).wait_recv()
        with mark("mix"):
            for g in range(G):
                v = r4[h, g].astype(f32)
                turned = pltpu.roll(v, MY, 1)
                rows = pl.ds(g * CB, CB)
                rr[h, :, rows, :] = jnp.where(low, v, turned).reshape(KB, CB, Q)
                ii[h, :, rows, :] = jnp.where(low, turned, v).reshape(KB, CB, Q)

            def mix_one(kx, carry):
                a = [None] * 4
                b = [None] * 4
                for c in range(C):
                    w = wv[slots[h], kx, c]
                    x = w * rr[h, kx, c : c + 1, :]
                    y = w * ii[h, kx, c : c + 1, :]
                    n = c % 4
                    a[n] = x if a[n] is None else a[n] + x
                    b[n] = y if b[n] is None else b[n] + y
                mf[h, kx] = ((a[0] + a[1]) + (a[2] + a[3])) - swapped((b[0] + b[1]) + (b[2] + b[3]))
                return carry

            for kx in range(KB):
                mix_one(kx, 0)
            r5[h, gy] = mf[h].reshape(KB * OB, Q).astype(bf16)
        staggered(h, send_mix)

    def send_mix(h):
        for _, peer, _ in gy_peers:
            remote(r5.at[h, gy], r5.at[h, gy], sent.at[7], r5s.at[h], "gy", peer).start()

    def step_back(h):
        part = r5.at[h, pl.ds(0, H - 1)]
        with mark("w5"):
            remote(part, part, sent.at[7], r5s.at[h], "gy", gy).wait_recv()
        with mark("back"):
            b6[h] = turn(x2, r5[h].reshape(H * KB * OB, Q)).reshape(b6.shape[1:])
        for _, peer, _ in gx_peers:
            remote(b6.at[h, peer], r6.at[h, gx], sent.at[8], r6s.at[h], "gx", peer).start()
        r6[h, gx] = b6[h, gx]

    def step_pass(h):
        part = r6.at[h, pl.ds(0, G - 1)]
        with mark("w6"):
            remote(part, part, sent.at[8], r6s.at[h], "gx", gx).wait_recv()
        remote(r6.at[h], r7.at[h], sent.at[9], r7s.at[h], "ga", other).start()

    def modes_of(ref, parity):
        parts = [ref[parity * HALF + i].reshape(C * XL, Q) for i in range(HALF)]
        return jnp.concatenate(parts, axis=1)

    def gather(ref, owner, parity):
        with mark("zdot"):
            y = modes_of(ref, parity)
            for j in range(NZC):
                span = slice(j * ZC * YL, (j + 1) * ZC * YL)
                acc[:, span] = acc[:, span] + dot(y, tb[2 * owner + parity, :, span])

    def arrived(h):
        with mark("w7"):
            remote(r6.at[h], r7.at[h], sent.at[9], r7s.at[h], "ga", other).wait_recv()

    for h in range(KZ):
        step_x(h)
    for h in range(KZ):
        step_y(h)
    for h in range(KZ):
        step_mix(h)
    for h in range(KZ):
        step_back(h)
    for h in range(HALF):
        step_pass(h)
    gather(r6, 0, 0)
    for h in range(HALF, KZ):
        step_pass(h)
    gather(r6, 0, 1)
    for h in range(HALF):
        arrived(h)
    gather(r7, 1, 0)
    for h in range(HALF, KZ):
        arrived(h)
    with mark("final"):
        last = modes_of(r7, 1)
        for j in range(NZC):
            span = slice(j * ZC * YL, (j + 1) * ZC * YL)
            done = gelu(acc[:, span] + dot(last, tb[3, :, span])).astype(bf16)
            for z in range(ZC):
                out[j * ZC + z] = done[:, z * YL : (z + 1) * YL].reshape(C, XL, YL)

    two = state.at[pl.ds(0, STEPS), :, pl.ds(0, 2)]
    for n, (axis, ref) in enumerate(
        (
            ("gy", ys),
            ("gx", xs),
            ("ga", two),
            ("ga", lift),
            ("gx", p2.at[:, pl.ds(0, G - 1)]),
            ("gy", q3.at[:, pl.ds(0, H - 1)]),
            ("gx", r4.at[:, pl.ds(0, G - 1)]),
            ("gy", r5.at[:, pl.ds(0, H - 1)]),
            ("gx", b6.at[:, pl.ds(0, G - 1)]),
            ("ga", r6),
        )
    ):
        remote(ref, ref, sent.at[n], sent.at[n], axis, lax.axis_index(axis)).wait_send()


def east_tables(G, H, XL, C):
    CB, KB, OB = C // G, MX // H, C // G
    length = G * XL
    k = np.arange(MX) - MX // 2
    ang = 2.0 * np.pi * ((k[:, None] * np.arange(length)[None, :]) % length) / length
    scale = 1.0 / math.sqrt(length)
    cos, sin = np.cos(ang) * scale, np.sin(ang) * scale
    cos[np.abs(cos) < 1e-12] = 0.0
    sin[np.abs(sin) < 1e-12] = 0.0

    def forward(t):
        t = t.reshape(H, KB, G, XL)
        full = np.einsum("hkgx,cd->hkcgdx", t, np.eye(CB))
        return full.reshape(H * CB * KB, G * CB * XL)

    def inverse(t):
        t = t.reshape(H, KB, G, XL)
        full = np.einsum("hkgx,op->goxhkp", t, np.eye(OB))
        return full.reshape(G * OB * XL, H * KB * OB)

    x1 = np.concatenate([forward(cos), forward(sin)], axis=0)
    x2 = np.concatenate([inverse(cos), -inverse(sin)], axis=0)
    return jnp.asarray(x1, bf16), jnp.asarray(x2, bf16)


def north_tables(H, YL, NZ):
    length = H * YL
    n = np.arange(MY) - MY // 2
    u = 2.0 * np.pi * ((np.arange(length)[:, None] * n[None, :]) % length) / length
    scale = 1.0 / math.sqrt(length * NZ)
    cu, su = np.cos(u) * scale, np.sin(u) * scale
    both = np.stack([np.concatenate([cu, -su], axis=1), np.concatenate([-su, -cu], axis=1)])
    both = both.reshape(2, H, YL, 2 * MY)
    return jnp.asarray(both.transpose(1, 0, 2, 3), f32), jnp.asarray(both.transpose(1, 0, 3, 2), f32)


def shards(fields, stiffness, lift_weight, lift_bias, mix_weight, spectral_weight, output_bias):
    G, H, A = (lax.axis_size(n) for n in ("gx", "gy", "ga"))
    _, NZL, NX, NY = fields.shape
    XL, YL = NX // 2, NY // 2
    C = lift_weight.shape[1]
    CB, KB, OB, KZ, Q = C // G, MX // H, C // G, MZ // A, 2 * MY
    NZ = NZL * A
    x1, x2 = east_tables(G, H, XL, C)
    ed, et = north_tables(H, YL, NZ)
    cfg = (G, H, A, C, CB, KB, OB, KZ, NZL, XL, YL)
    vmem_bytes = 67043328 - 2 * NZL * C * XL * YL
    hbm = pl.BlockSpec(memory_space=pltpu.HBM)
    NZC, HALF = DEPTH_CHUNKS, KZ // 2
    ZW = NZL // NZC * YL
    dma = pltpu.SemaphoreType.DMA
    V = pltpu.VMEM
    return pl.pallas_call(
        functools.partial(layer_kernel, cfg),
        out_shape=V((NZL, C, XL, YL), bf16),
        in_specs=[hbm] * 11,
        out_specs=pl.BlockSpec(memory_space=V),
        scratch_shapes=[
            V((STEPS + 1, 5, NZL + 2, NX, NY), f32),
            V((NZL, NX, NY), f32),
            V((STEPS, 2, 5, NZL, NY), bf16),
            V((STEPS, 2, 5, NZL, NY), bf16),
            V((STEPS, 2, 5, NZL * NX), f32),
            V((STEPS, 2, 5, NZL * NX), f32),
            V((5 * NZL * NX, 2 * NY), bf16),
            V((5 * NZL * NX, YL), f32),
            V(ed.shape[1:], f32),
            V(et.shape[1:], f32),
            V(x1.shape, bf16),
            V(x2.shape, bf16),
            V(spectral_weight.shape, f32),
            V(lift_weight.shape, f32),
            V((1, C), f32),
            V(mix_weight.shape, bf16),
            V((1, C), f32),
            V((C * XL, 16 * XL), bf16),
            V((NZC, 16 * XL, ZW), bf16),
            V((NZC, C * XL, ZW), bf16),
            V((NZC, C * XL, ZW), bf16),
            V((2, NZC, C * XL, ZW), bf16),
            V((2, NZC, ZW, HALF * Q), bf16),
            V((2 * A, HALF * Q, NZL * YL), bf16),
            V((KZ, G, CB * XL, Q), bf16),
            V((KZ, G, CB * XL, Q), bf16),
            V((KZ, H, CB * KB, Q), bf16),
            V((KZ, H - 1, CB * KB, Q), bf16),
            V((KZ, CB * KB, Q), bf16),
            V((KZ, G, CB * KB, Q), bf16),
            V((KZ, KB, C, Q), f32),
            V((KZ, KB, C, Q), f32),
            V((KZ, KB, OB, Q), f32),
            V((KZ, H, KB * OB, Q), bf16),
            V((KZ, G, OB * XL, Q), bf16),
            V((KZ, G, OB * XL, Q), bf16),
            V((KZ, G, OB * XL, Q), bf16),
            V((C * XL, NZL * YL), f32),
            dma((15,)), dma((10,)), dma((STEPS, 3)),
            dma((NZC,)), dma((KZ,)), dma((KZ,)), dma((KZ,)), dma((KZ,)), dma((KZ,)), dma((KZ,)),
        ],
        compiler_params=pltpu.CompilerParams(collective_id=0, has_side_effects=True, vmem_limit_bytes=vmem_bytes),
    )(
        fields, stiffness, ed, et, x1, x2, spectral_weight,
        lift_weight, lift_bias[None, :], mix_weight, output_bias[None, :],
    )


def solution(mesh):
    placed = (
        P(None, "ga", "gx", "gy"),
        P("ga", "gx", "gy"),
        P(),
        P(),
        P(),
        P("ga", "gy", None, "gx", None),
        P(),
    )
    return jax.shard_map(
        shards, mesh=mesh, in_specs=placed, out_specs=P("ga", None, "gx", "gy"), check_vma=False
    )
```

```python
import math

import contextlib
import functools
import jax
import jax.numpy as jnp
import numpy as np
from jax import lax
from jax.experimental import pallas as pl
from jax.experimental.pallas import tpu as pltpu
from jax.sharding import PartitionSpec as P

STEPS = 3
MX = 32
MY = 64
MZ = 8
DEPTH_CHUNKS = 4


courant_half = 0.1
smooth_half = 0.15
mean_flow = (0.3, -0.2, 0.1)
highest = lax.Precision.HIGHEST


MESH = pl.DeviceIdType.MESH
f32 = jnp.float32
bf16 = jnp.bfloat16


def gelu(v):
    scale = math.sqrt(2.0 / math.pi)
    half = 0.5 * v
    return half + half * jnp.tanh(v * (scale + (0.044715 * scale) * (v * v)))


def mark(name):
    return contextlib.nullcontext()


def swapped(v):
    sign = jnp.where(lax.broadcasted_iota(jnp.int32, v.shape, 1) < MY, 1.0, -1.0)
    return pltpu.roll(v, MY, 1) * sign


def dot(a, b, dims=((1,), (0,))):
    return lax.dot_general(a, b, (dims, ((), ())), preferred_element_type=f32)


def line_peers(axis):
    count = lax.axis_size(axis)
    me = lax.axis_index(axis)
    order = []
    for j in range(count - 1):
        down, up = count - 1 - j, j
        down = jnp.where(down <= me, down - 1, down)
        up = jnp.where(up >= me, up + 1, up)
        order.append(jnp.where(me < count // 2, down, up))
    return me, order


def square_peers(axis):
    count = lax.axis_size(axis)
    me = lax.axis_index(axis)
    if count != 4:
        return line_peers(axis)
    flip_x = me + 1 - 2 * lax.rem(me, 2)
    return me, [3 - me, 3 - flip_x, flip_x]


def remote(src, dst, send, recv, axis, peer):
    return pltpu.make_async_remote_copy(
        src_ref=src,
        dst_ref=dst,
        send_sem=send,
        recv_sem=recv,
        device_id={axis: peer},
        device_id_type=MESH,
    )


def stencil_step(state, target, stiff, xr, yr, dims):
    NZ, NX, NY = dims
    eye = lax.broadcasted_iota(jnp.int32, (NZ * NX, NZ * NX), 0) == lax.broadcasted_iota(
        jnp.int32, (NZ * NX, NZ * NX), 1
    )
    columns = [
        [
            jnp.sum(
                jnp.where(eye, jnp.broadcast_to(yr[side, f : f + 1, :], eye.shape), 0.0),
                axis=1,
                keepdims=True,
            )
            for f in range(5)
        ]
        for side in range(2)
    ]
    weights = [
        ((smooth_half + courant_half * flow) / courant_half, (smooth_half - courant_half * flow) / courant_half)
        for flow in mean_flow
    ]
    keep = (1.0 - 6.0 * smooth_half) / courant_half
    for z in range(NZ):
        near = []
        for f in range(5):
            c = state[f, z + 1]
            span = slice(z * NX, (z + 1) * NX)
            xl = shifted(c, xr[0, f, z : z + 1, :].astype(f32), 0, 1, 8)
            xu = shifted(c, xr[1, f, z : z + 1, :].astype(f32), 0, -1, 8)
            yl = shifted(c, columns[0][f][span], 1, 1, 128)
            yu = shifted(c, columns[1][f][span], 1, -1, 128)
            near.append((c, xl, xu, yl, yu, state[f, z], state[f, z + 2]))
        diverge = (
            (near[1][2] - near[1][1]) + (near[2][4] - near[2][3]) + (near[3][6] - near[3][5])
        )
        p = near[4]
        coupling = (diverge, p[2] - p[1], p[4] - p[3], p[6] - p[5], stiff[z] * diverge)
        for f in range(5):
            c, xl, xu, yl, yu, zl, zu = near[f]
            total = c if abs(keep - 1.0) < 1e-12 else keep * c
            for (low, high), lower, upper in zip(weights, (xl, yl, zl), (xu, yu, zu)):
                total = total + (low * lower + high * upper)
            target[f, z + 1] = total - coupling[f]


def shifted(c, halo, axis, step, tile):
    count = c.shape[axis] // tile
    pieces = [lax.slice_in_dim(c, i * tile, (i + 1) * tile, axis=axis) for i in range(count)]
    rolled = [pltpu.roll(piece, step % tile, axis) for piece in pieces]
    edge = 0 if step > 0 else tile - 1
    at_edge = lax.broadcasted_iota(jnp.int32, pieces[0].shape, axis) == edge
    before = [halo] + rolled[:-1] if step > 0 else rolled[1:] + [halo]
    return jnp.concatenate([jnp.where(at_edge, b, r) for b, r in zip(before, rolled)], axis=axis)


def layer_kernel(
    cfg,
    fields_hbm, stiff_hbm, ed_hbm, et_hbm, x1_hbm, x2_hbm, w_hbm, lw_hbm, lb_hbm, mix_hbm, bias_hbm,
    out,
    state, stiff, xs, xr, ys, yr, pairs, filt, ed, et, x1, x2, wv, lw, lb, mix, bias_row, wide_lift,
    spread_in, lift, lift_in, both, tf, tb, p2, r2, q3, r3, c4, r4, rr, ii, mf, r5, b6, r6, r7, acc,
    local, sent, hr, r1s, r2s, r3s, r4s, r5s, r6s, r7s,
):
    G, H, A, C, CB, KB, OB, KZ, NZL, XL, YL = cfg
    Q = 2 * MY
    NX, NY = 2 * XL, 2 * YL
    gx, gx_peers = square_peers("gx")
    gy, gy_peers = line_peers("gy")
    ga = lax.axis_index("ga")
    other = lax.rem(ga + 1, A)
    barrier = pltpu.get_barrier_semaphore()
    for axis, group in (("gx", gx_peers), ("gy", gy_peers)):
        for peer in group:
            pl.semaphore_signal(barrier, inc=1, device_id={axis: peer}, device_id_type=MESH)
    pl.semaphore_signal(barrier, inc=1, device_id={"ga": other}, device_id_type=MESH)
    loads = [
        pltpu.make_async_copy(source, target, local.at[n])
        for n, (source, target) in enumerate(
            (
                (fields_hbm, state.at[0, :, pl.ds(1, NZL)]),
                (stiff_hbm, stiff),
                (ed_hbm.at[gy], ed),
                (et_hbm.at[gy], et),
                (x1_hbm, x1),
                (x2_hbm, x2),
                (w_hbm, wv),
                (lw_hbm, lw),
                (lb_hbm, lb),
                (mix_hbm, mix),
                (bias_hbm, bias_row),
            )
        )
    ]
    first, loads = loads[0], loads[1:]
    first.start()

    HALF = KZ // 2
    NZC = DEPTH_CHUNKS
    ZC = NZL // NZC
    NZ = NZL * A
    slots = list(range(0, KZ, 2)) + list(range(1, KZ, 2))

    def own(values):
        picked = jnp.float32(values[0])
        for n in range(1, A):
            picked = jnp.where(ga == n, jnp.float32(values[n]), picked)
        return picked

    def angles(z, owner, k):
        v = [
            2.0 * math.pi * ((((n + owner) % A * KZ + k) * (n * NZL + z)) % NZ) / NZ for n in range(A)
        ]
        return own([math.cos(x) for x in v]), own([math.sin(x) for x in v])

    def build_table():
        loads[1].wait()
        loads[2].wait()
        for z in range(NZL):
            for owner in range(A):
                for j, k in enumerate(slots):
                    cos, sin = angles(z, owner, k)
                    span = slice((j % HALF) * Q, (j % HALF + 1) * Q)
                    if owner == 0:
                        block = ed[0] * cos + ed[1] * sin
                        rows = slice(z % ZC * YL, (z % ZC + 1) * YL)
                        tf[j // HALF, z // ZC, rows, span] = block.astype(bf16)
                    block = et[0] * cos + et[1] * sin
                    tb[2 * owner + j // HALF, span, z * YL : (z + 1) * YL] = block.astype(bf16)

    spread = jnp.where(
        lax.broadcasted_iota(jnp.int32, (C * XL, C), 0) // XL
        == lax.broadcasted_iota(jnp.int32, (C * XL, C), 1),
        1.0,
        0.0,
    )

    def tall(values):
        return jnp.sum(spread * values, axis=1, keepdims=True)

    def build_lift():
        for n in (6, 7):
            loads[n].wait()
        row = lax.broadcasted_iota(jnp.int32, (C * XL, 16 * XL), 0)
        lane = lax.broadcasted_iota(jnp.int32, (C * XL, 16 * XL), 1)
        group = lane // XL
        table = jnp.zeros((C * XL, 16 * XL), f32)
        for f in range(6):
            values = tall(lw[f : f + 1, :] if f < 5 else lb[...])
            high = values.astype(bf16).astype(f32)
            rest = values - high
            if f < 5:
                table = jnp.where((group == f) | (group == 5 + f), high, table)
                table = jnp.where(group == 10 + f, rest, table)
        same = lax.rem(row, XL) == lax.rem(lane, XL)
        table = jnp.where(same & (group < 15), table, 0.0)
        table = jnp.where(lane == 15 * XL, high, table)
        table = jnp.where(lane == 15 * XL + 1, rest, table)
        wide_lift[...] = table.astype(bf16)

    with mark("ld0"):
        first.wait()
    eye = lax.broadcasted_iota(jnp.int32, (NZL * NX, NZL * NX), 0) == lax.broadcasted_iota(
        jnp.int32, (NZL * NX, NZL * NX), 1
    )
    for t in range(STEPS):
        now = state.at[t]
        with mark("pack%d" % t):
            for side, (edge_x, edge_y) in enumerate(((NX - 1, NY - 1), (0, 0))):
                for f in range(5):
                    for z in range(NZL):
                        row = now[f, z + 1, edge_x : edge_x + 1, :]
                        xs[t, side, f, z : z + 1, :] = row.astype(bf16)
                    column = now[f, 1 : NZL + 1, :, edge_y : edge_y + 1].reshape(NZL * NX, 1)
                    ys[t, side, f : f + 1, :] = jnp.sum(
                        jnp.where(eye, jnp.broadcast_to(column, eye.shape), 0.0),
                        axis=0,
                        keepdims=True,
                    )
        if t == 0:
            with mark("barrier"):
                pl.semaphore_wait(barrier, (G - 1) + (H - 1) + 1)
        for side in range(2):
            ty = lax.rem(gy + H + (1 if side == 0 else -1), H)
            remote(ys.at[t, side], yr.at[t, side], sent.at[0], hr.at[t, 0], "gy", ty).start()
        for turn_of in range(2):
            side = lax.rem(gx + 1 + turn_of, 2)
            tx = lax.rem(gx + G + 1 - 2 * side, G)
            remote(xs.at[t, side], xr.at[t, side], sent.at[1], hr.at[t, 1], "gx", tx).start()
        for plane, halo in ((NZL, 0), (1, NZL + 1)):
            remote(now.at[:, plane], now.at[:, halo], sent.at[2], hr.at[t, 2], "ga", other).start()
        if t == 0:
            for load in loads:
                load.start()
            with mark("table"):
                build_table()
                loads[0].wait()
        if t == STEPS - 1:
            with mark("buildlift"):
                build_lift()
        with mark("halo%d" % t):
            remote(ys.at[t], yr.at[t], sent.at[0], hr.at[t, 0], "gy", gy).wait_recv()
            remote(xs.at[t], xr.at[t], sent.at[1], hr.at[t, 1], "gx", gx).wait_recv()
            two = now.at[:, pl.ds(0, 2)]
            remote(two, two, sent.at[2], hr.at[t, 2], "ga", other).wait_recv()
        with mark("stencil%d" % t):
            stencil_step(now, state.at[t + 1], stiff, xr.at[t], yr.at[t], (NZL, NX, NY))

    with mark("filter"):
        twin = lax.rem(lax.broadcasted_iota(jnp.int32, (2 * NY, YL), 0), NY) // 2
        twin = jnp.where(twin == lax.broadcasted_iota(jnp.int32, (2 * NY, YL), 1), 1.0, 0.0)
        for f in range(5):
            v = state[STEPS, f, 1 : NZL + 1].reshape(NZL * NX, NY)
            high = v.astype(bf16)
            rows = pl.ds(f * NZL * NX, NZL * NX)
            pairs[rows, :NY] = high
            pairs[rows, NY:] = (v - high.astype(f32)).astype(bf16)
        for rows in (pl.ds(0, 5 * NZL * XL), pl.ds(5 * NZL * XL, 5 * NZL * XL)):
            filt[rows] = dot(pairs[rows], twin.astype(bf16))

        def mean(f, z):
            start = (f * NZL + z) * NX
            both_rows = filt[pl.ds(start, XL, stride=2), :] + filt[pl.ds(start + 1, XL, stride=2), :]
            return both_rows * (0.25 * courant_half**STEPS)

        for z in range(NZL):
            v = jnp.concatenate([mean(f, z) for f in range(5)], axis=0)
            high = v.astype(bf16).astype(f32)
            v = jnp.concatenate([high, v - high, high, jnp.ones((XL, YL), f32)], axis=0)
            span = slice(z % ZC * YL, (z % ZC + 1) * YL)
            spread_in[z // ZC, :, span] = v.astype(bf16)

    with mark("lift"):
        for n in range(0, NZC, 2):
            for i in range(n, n + 2):
                lift[i] = gelu(dot(wide_lift[...], spread_in[i])).astype(bf16)
            for i in range(n, n + 2):
                remote(lift.at[i], lift_in.at[i], sent.at[3], r1s.at[i], "ga", other).start()
    for n in range(NZC):
        with mark("w1"):
            remote(lift.at[n], lift_in.at[n], sent.at[3], r1s.at[n], "ga", other).wait_recv()
        with mark("sumdiff"):
            mine, theirs = lift[n], lift_in[n]
            both[0, n] = mine + theirs
            both[1, n] = mine - theirs

    with mark("dot1"):
        for parity in range(2):
            modes = dot(both[parity, 0], tf[parity, 0])
            for n in range(1, NZC):
                modes = modes + dot(both[parity, n], tf[parity, n])
            modes = modes.astype(bf16)
            for i in range(HALF):
                p2[parity * HALF + i] = modes[:, i * Q : (i + 1) * Q].reshape(p2.shape[1:])
    for h in range(KZ):
        for peer in gx_peers:
            remote(p2.at[h, peer], r2.at[h, gx], sent.at[4], r2s.at[h], "gx", peer).start()
    for h in range(KZ):
        r2[h, gx] = p2[h, gx]

    with mark("direct"):
        loads[8].wait()
        loads[9].wait()
        bias = tall(bias_row[...])
        wide = dot(spread.astype(bf16), mix[...], ((1,), (1,))).astype(bf16)
        wide = dot(wide, spread.astype(bf16), ((1,), (1,)))
        same = lax.rem(lax.broadcasted_iota(jnp.int32, wide.shape, 0), XL) == lax.rem(
            lax.broadcasted_iota(jnp.int32, wide.shape, 1), XL
        )
        mixk = jnp.where(same, wide, 0.0).astype(bf16)
        for j in range(NZC):
            span = slice(j * ZC * YL, (j + 1) * ZC * YL)
            acc[:, span] = dot(mixk, lift[j]) + bias
        loads[3].wait()
        loads[4].wait()
        loads[5].wait()

    def turn(x, v):
        rows = x.shape[0] // 2
        return (dot(x[:rows], v) + swapped(dot(x[rows:], v))).astype(bf16)

    def staggered(h, send, size):
        @pl.when(ga == 0)
        def _():
            send(h)

        if (h + 1) % size == 0:

            @pl.when(ga != 0)
            def _():
                for i in range(h + 1 - size, h + 1):
                    send(i)

    def step_x(h):
        part = r2.at[h, pl.ds(0, G - 1)]
        with mark("w2"):
            remote(part, part, sent.at[4], r2s.at[h], "gx", gx).wait_recv()
        with mark("xdot"):
            q3[h] = turn(x1, r2[h].reshape(C * XL, Q)).reshape(q3.shape[1:])
        staggered(h, send_x, KZ)

    def send_x(h):
        for peer in gy_peers:
            remote(q3.at[h, peer], r3.at[h, gy], sent.at[5], r3s.at[h], "gy", peer).start()

    def step_y(h):
        with mark("w3"):
            part = r3.at[h, pl.ds(0, H - 1)]
            remote(part, part, sent.at[5], r3s.at[h], "gy", gy).wait_recv()
        total = q3[h, gy].astype(f32)
        for peer in gy_peers:
            total = total + r3[h, peer].astype(f32)
        c4[h] = total.astype(bf16)
        for peer in gx_peers:
            remote(c4.at[h], r4.at[h, gx], sent.at[6], r4s.at[h], "gx", peer).start()
        r4[h, gx] = c4[h]

    low = lax.broadcasted_iota(jnp.int32, (CB * KB, Q), 1) < MY

    def step_mix(h):
        part = r4.at[h, pl.ds(0, G - 1)]
        with mark("w4"):
            remote(part, part, sent.at[6], r4s.at[h], "gx", gx).wait_recv()
        with mark("mix"):
            for g in range(G):
                v = r4[h, g].astype(f32)
                turned = pltpu.roll(v, MY, 1)
                rows = pl.ds(g * CB, CB)
                rr[h, :, rows, :] = jnp.where(low, v, turned).reshape(KB, CB, Q)
                ii[h, :, rows, :] = jnp.where(low, turned, v).reshape(KB, CB, Q)

            def mix_one(kx, carry):
                a = [None] * 4
                b = [None] * 4
                for c in range(C):
                    w = wv[slots[h], kx, c]
                    x = w * rr[h, kx, c : c + 1, :]
                    y = w * ii[h, kx, c : c + 1, :]
                    n = c % 4
                    a[n] = x if a[n] is None else a[n] + x
                    b[n] = y if b[n] is None else b[n] + y
                mf[h, kx] = ((a[0] + a[1]) + (a[2] + a[3])) - swapped((b[0] + b[1]) + (b[2] + b[3]))
                return carry

            for kx in range(KB):
                mix_one(kx, 0)
            r5[h, gy] = mf[h].reshape(KB * OB, Q).astype(bf16)
        staggered(h, send_mix, HALF)

    def send_mix(h):
        for peer in gy_peers:
            remote(r5.at[h, gy], r5.at[h, gy], sent.at[7], r5s.at[h], "gy", peer).start()

    def step_back(h):
        part = r5.at[h, pl.ds(0, H - 1)]
        with mark("w5"):
            remote(part, part, sent.at[7], r5s.at[h], "gy", gy).wait_recv()
        with mark("back"):
            b6[h] = turn(x2, r5[h].reshape(H * KB * OB, Q)).reshape(b6.shape[1:])
        for peer in gx_peers:
            remote(b6.at[h, peer], r6.at[h, gx], sent.at[8], r6s.at[h], "gx", peer).start()
        r6[h, gx] = b6[h, gx]

    def step_pass(h):
        part = r6.at[h, pl.ds(0, G - 1)]
        with mark("w6"):
            remote(part, part, sent.at[8], r6s.at[h], "gx", gx).wait_recv()
        remote(r6.at[h], r7.at[h], sent.at[9], r7s.at[h], "ga", other).start()

    def modes_of(ref, parity):
        parts = [ref[parity * HALF + i].reshape(C * XL, Q) for i in range(HALF)]
        return jnp.concatenate(parts, axis=1)

    def gather(ref, owner, parity):
        with mark("zdot"):
            y = modes_of(ref, parity)
            for j in range(NZC):
                span = slice(j * ZC * YL, (j + 1) * ZC * YL)
                acc[:, span] = acc[:, span] + dot(y, tb[2 * owner + parity, :, span])

    def arrived(h):
        with mark("w7"):
            remote(r6.at[h], r7.at[h], sent.at[9], r7s.at[h], "ga", other).wait_recv()

    for h in range(KZ):
        step_x(h)
    for h in range(KZ):
        step_y(h)
    for h in range(KZ):
        step_mix(h)
    for h in range(KZ):
        step_back(h)
    for h in range(HALF):
        step_pass(h)
    gather(r6, 0, 0)
    for h in range(HALF, KZ):
        step_pass(h)
    gather(r6, 0, 1)
    for h in range(HALF):
        arrived(h)
    gather(r7, 1, 0)
    for h in range(HALF, KZ):
        arrived(h)
    with mark("final"):
        last = modes_of(r7, 1)
        for j in range(NZC):
            span = slice(j * ZC * YL, (j + 1) * ZC * YL)
            done = gelu(acc[:, span] + dot(last, tb[3, :, span])).astype(bf16)
            for z in range(ZC):
                out[j * ZC + z] = done[:, z * YL : (z + 1) * YL].reshape(C, XL, YL)

    two = state.at[pl.ds(0, STEPS), :, pl.ds(0, 2)]
    for n, (axis, ref) in enumerate(
        (
            ("gy", ys),
            ("gx", xs),
            ("ga", two),
            ("ga", lift),
            ("gx", p2.at[:, pl.ds(0, G - 1)]),
            ("gy", q3.at[:, pl.ds(0, H - 1)]),
            ("gx", r4.at[:, pl.ds(0, G - 1)]),
            ("gy", r5.at[:, pl.ds(0, H - 1)]),
            ("gx", b6.at[:, pl.ds(0, G - 1)]),
            ("ga", r6),
        )
    ):
        remote(ref, ref, sent.at[n], sent.at[n], axis, lax.axis_index(axis)).wait_send()


def east_tables(G, H, XL, C):
    CB, KB, OB = C // G, MX // H, C // G
    length = G * XL
    k = np.arange(MX) - MX // 2
    ang = 2.0 * np.pi * ((k[:, None] * np.arange(length)[None, :]) % length) / length
    scale = 1.0 / math.sqrt(length)
    cos, sin = np.cos(ang) * scale, np.sin(ang) * scale
    cos[np.abs(cos) < 1e-12] = 0.0
    sin[np.abs(sin) < 1e-12] = 0.0

    def forward(t):
        t = t.reshape(H, KB, G, XL)
        full = np.einsum("hkgx,cd->hkcgdx", t, np.eye(CB))
        return full.reshape(H * CB * KB, G * CB * XL)

    def inverse(t):
        t = t.reshape(H, KB, G, XL)
        full = np.einsum("hkgx,op->goxhkp", t, np.eye(OB))
        return full.reshape(G * OB * XL, H * KB * OB)

    x1 = np.concatenate([forward(cos), forward(sin)], axis=0)
    x2 = np.concatenate([inverse(cos), -inverse(sin)], axis=0)
    return jnp.asarray(x1, bf16), jnp.asarray(x2, bf16)


def north_tables(H, YL, NZ):
    length = H * YL
    n = np.arange(MY) - MY // 2
    u = 2.0 * np.pi * ((np.arange(length)[:, None] * n[None, :]) % length) / length
    scale = 1.0 / math.sqrt(length * NZ)
    cu, su = np.cos(u) * scale, np.sin(u) * scale
    both = np.stack([np.concatenate([cu, -su], axis=1), np.concatenate([-su, -cu], axis=1)])
    both = both.reshape(2, H, YL, 2 * MY)
    return jnp.asarray(both.transpose(1, 0, 2, 3), f32), jnp.asarray(both.transpose(1, 0, 3, 2), f32)


def shards(fields, stiffness, lift_weight, lift_bias, mix_weight, spectral_weight, output_bias):
    G, H, A = (lax.axis_size(n) for n in ("gx", "gy", "ga"))
    _, NZL, NX, NY = fields.shape
    XL, YL = NX // 2, NY // 2
    C = lift_weight.shape[1]
    CB, KB, OB, KZ, Q = C // G, MX // H, C // G, MZ // A, 2 * MY
    NZ = NZL * A
    x1, x2 = east_tables(G, H, XL, C)
    ed, et = north_tables(H, YL, NZ)
    cfg = (G, H, A, C, CB, KB, OB, KZ, NZL, XL, YL)
    vmem_bytes = 67043328 - 2 * NZL * C * XL * YL
    hbm = pl.BlockSpec(memory_space=pltpu.HBM)
    NZC, HALF = DEPTH_CHUNKS, KZ // 2
    ZW = NZL // NZC * YL
    dma = pltpu.SemaphoreType.DMA
    V = pltpu.VMEM
    return pl.pallas_call(
        functools.partial(layer_kernel, cfg),
        out_shape=V((NZL, C, XL, YL), bf16),
        in_specs=[hbm] * 11,
        out_specs=pl.BlockSpec(memory_space=V),
        scratch_shapes=[
            V((STEPS + 1, 5, NZL + 2, NX, NY), f32),
            V((NZL, NX, NY), f32),
            V((STEPS, 2, 5, NZL, NY), bf16),
            V((STEPS, 2, 5, NZL, NY), bf16),
            V((STEPS, 2, 5, NZL * NX), f32),
            V((STEPS, 2, 5, NZL * NX), f32),
            V((5 * NZL * NX, 2 * NY), bf16),
            V((5 * NZL * NX, YL), f32),
            V(ed.shape[1:], f32),
            V(et.shape[1:], f32),
            V(x1.shape, bf16),
            V(x2.shape, bf16),
            V(spectral_weight.shape, f32),
            V(lift_weight.shape, f32),
            V((1, C), f32),
            V(mix_weight.shape, bf16),
            V((1, C), f32),
            V((C * XL, 16 * XL), bf16),
            V((NZC, 16 * XL, ZW), bf16),
            V((NZC, C * XL, ZW), bf16),
            V((NZC, C * XL, ZW), bf16),
            V((2, NZC, C * XL, ZW), bf16),
            V((2, NZC, ZW, HALF * Q), bf16),
            V((2 * A, HALF * Q, NZL * YL), bf16),
            V((KZ, G, CB * XL, Q), bf16),
            V((KZ, G, CB * XL, Q), bf16),
            V((KZ, H, CB * KB, Q), bf16),
            V((KZ, H, CB * KB, Q), bf16),
            V((KZ, CB * KB, Q), bf16),
            V((KZ, G, CB * KB, Q), bf16),
            V((KZ, KB, C, Q), f32),
            V((KZ, KB, C, Q), f32),
            V((KZ, KB, OB, Q), f32),
            V((KZ, H, KB * OB, Q), bf16),
            V((KZ, G, OB * XL, Q), bf16),
            V((KZ, G, OB * XL, Q), bf16),
            V((KZ, G, OB * XL, Q), bf16),
            V((C * XL, NZL * YL), f32),
            dma((11,)), dma((10,)), dma((STEPS, 3)),
            dma((NZC,)), dma((KZ,)), dma((KZ,)), dma((KZ,)), dma((KZ,)), dma((KZ,)), dma((KZ,)),
        ],
        compiler_params=pltpu.CompilerParams(collective_id=0, has_side_effects=True, vmem_limit_bytes=vmem_bytes),
    )(
        fields, stiffness, ed, et, x1, x2, spectral_weight,
        lift_weight, lift_bias[None, :], mix_weight, output_bias[None, :],
    )


def solution(mesh):
    placed = (
        P(None, "ga", "gx", "gy"),
        P("ga", "gx", "gy"),
        P(),
        P(),
        P(),
        P("ga", "gy", None, "gx", None),
        P(),
    )
    return jax.shard_map(
        shards, mesh=mesh, in_specs=placed, out_specs=P("ga", None, "gx", "gy"), check_vma=False
    )
```

```python
import math

import contextlib
import functools
import jax
import jax.numpy as jnp
import numpy as np
from jax import lax
from jax.experimental import pallas as pl
from jax.experimental.pallas import tpu as pltpu
from jax.sharding import PartitionSpec as P

STEPS = 3
MX = 32
MY = 64
MZ = 8
DEPTH_CHUNKS = 4


courant_half = 0.1
smooth_half = 0.15
mean_flow = (0.3, -0.2, 0.1)
highest = lax.Precision.HIGHEST


MESH = pl.DeviceIdType.MESH
f32 = jnp.float32
bf16 = jnp.bfloat16


def gelu(v):
    scale = math.sqrt(2.0 / math.pi)
    half = 0.5 * v
    return half + half * jnp.tanh(v * (scale + (0.044715 * scale) * (v * v)))


def swapped(v):
    sign = jnp.where(lax.broadcasted_iota(jnp.int32, v.shape, 1) < MY, 1.0, -1.0)
    return pltpu.roll(v, MY, 1) * sign


def dot(a, b, dims=((1,), (0,))):
    return lax.dot_general(a, b, (dims, ((), ())), preferred_element_type=f32)


def line_peers(axis):
    count = lax.axis_size(axis)
    me = lax.axis_index(axis)
    order = []
    for j in range(count - 1):
        down, up = count - 1 - j, j
        down = jnp.where(down <= me, down - 1, down)
        up = jnp.where(up >= me, up + 1, up)
        order.append(jnp.where(me < count // 2, down, up))
    return me, order


def square_peers(axis):
    count = lax.axis_size(axis)
    me = lax.axis_index(axis)
    if count != 4:
        return line_peers(axis)
    flip_x = me + 1 - 2 * lax.rem(me, 2)
    return me, [3 - me, 3 - flip_x, flip_x]


def remote(src, dst, send, recv, axis, peer):
    return pltpu.make_async_remote_copy(
        src_ref=src,
        dst_ref=dst,
        send_sem=send,
        recv_sem=recv,
        device_id={axis: peer},
        device_id_type=MESH,
    )


def stencil_step(state, target, stiff, xr, yr, dims):
    NZ, NX, NY = dims
    eye = lax.broadcasted_iota(jnp.int32, (NZ * NX, NZ * NX), 0) == lax.broadcasted_iota(
        jnp.int32, (NZ * NX, NZ * NX), 1
    )
    columns = [
        [
            jnp.sum(
                jnp.where(eye, jnp.broadcast_to(yr[side, f : f + 1, :], eye.shape), 0.0),
                axis=1,
                keepdims=True,
            )
            for f in range(5)
        ]
        for side in range(2)
    ]
    weights = [
        ((smooth_half + courant_half * flow) / courant_half, (smooth_half - courant_half * flow) / courant_half)
        for flow in mean_flow
    ]
    keep = (1.0 - 6.0 * smooth_half) / courant_half
    for z in range(NZ):
        near = []
        for f in range(5):
            c = state[f, z + 1]
            span = slice(z * NX, (z + 1) * NX)
            xl = shifted(c, xr[0, f, z : z + 1, :].astype(f32), 0, 1, 8)
            xu = shifted(c, xr[1, f, z : z + 1, :].astype(f32), 0, -1, 8)
            yl = shifted(c, columns[0][f][span], 1, 1, 128)
            yu = shifted(c, columns[1][f][span], 1, -1, 128)
            near.append((c, xl, xu, yl, yu, state[f, z], state[f, z + 2]))
        diverge = (
            (near[1][2] - near[1][1]) + (near[2][4] - near[2][3]) + (near[3][6] - near[3][5])
        )
        p = near[4]
        coupling = (diverge, p[2] - p[1], p[4] - p[3], p[6] - p[5], stiff[z] * diverge)
        for f in range(5):
            c, xl, xu, yl, yu, zl, zu = near[f]
            total = c if abs(keep - 1.0) < 1e-12 else keep * c
            for (low, high), lower, upper in zip(weights, (xl, yl, zl), (xu, yu, zu)):
                total = total + (low * lower + high * upper)
            target[f, z + 1] = total - coupling[f]


def shifted(c, halo, axis, step, tile):
    count = c.shape[axis] // tile
    pieces = [lax.slice_in_dim(c, i * tile, (i + 1) * tile, axis=axis) for i in range(count)]
    rolled = [pltpu.roll(piece, step % tile, axis) for piece in pieces]
    edge = 0 if step > 0 else tile - 1
    at_edge = lax.broadcasted_iota(jnp.int32, pieces[0].shape, axis) == edge
    before = [halo] + rolled[:-1] if step > 0 else rolled[1:] + [halo]
    return jnp.concatenate([jnp.where(at_edge, b, r) for b, r in zip(before, rolled)], axis=axis)


def layer_kernel(
    cfg,
    fields_hbm, stiff_hbm, ed_hbm, et_hbm, x1_hbm, x2_hbm, w_hbm, lw_hbm, lb_hbm, mix_hbm, bias_hbm,
    out,
    state, stiff, xs, xr, ys, yr, pairs, filt, ed, et, x1, x2, wv, lw, lb, mix, bias_row, wide_lift,
    spread_in, lift, lift_in, both, tf, tb, p2, r2, q3, r3, c4, r4, rr, ii, mf, r5, b6, r6, r7, acc,
    local, sent, hr, r1s, r2s, r3s, r4s, r5s, r6s, r7s, wall,
):
    G, H, A, C, CB, KB, OB, KZ, NZL, XL, YL = cfg
    Q = 2 * MY
    NX, NY = 2 * XL, 2 * YL

    def fence():
        @pl.when(lax.axis_index("ga") < 0)
        def _():
            wall[...] = jnp.zeros_like(wall)

    @contextlib.contextmanager
    def mark(name):
        fence()
        yield
        fence()

    gx, gx_peers = square_peers("gx")
    gy, gy_peers = line_peers("gy")
    ga = lax.axis_index("ga")
    other = lax.rem(ga + 1, A)
    barrier = pltpu.get_barrier_semaphore()
    for axis, group in (("gx", gx_peers), ("gy", gy_peers)):
        for peer in group:
            pl.semaphore_signal(barrier, inc=1, device_id={axis: peer}, device_id_type=MESH)
    pl.semaphore_signal(barrier, inc=1, device_id={"ga": other}, device_id_type=MESH)
    loads = [
        pltpu.make_async_copy(source, target, local.at[n])
        for n, (source, target) in enumerate(
            (
                (fields_hbm, state.at[0, :, pl.ds(1, NZL)]),
                (stiff_hbm, stiff),
                (ed_hbm.at[gy], ed),
                (et_hbm.at[gy], et),
                (x1_hbm, x1),
                (x2_hbm, x2),
                (w_hbm, wv),
                (lw_hbm, lw),
                (lb_hbm, lb),
                (mix_hbm, mix),
                (bias_hbm, bias_row),
            )
        )
    ]
    first, loads = loads[0], loads[1:]
    first.start()

    HALF = KZ // 2
    NZC = DEPTH_CHUNKS
    ZC = NZL // NZC
    NZ = NZL * A
    slots = list(range(0, KZ, 2)) + list(range(1, KZ, 2))

    def own(values):
        picked = jnp.float32(values[0])
        for n in range(1, A):
            picked = jnp.where(ga == n, jnp.float32(values[n]), picked)
        return picked

    def angles(z, owner, k):
        v = [
            2.0 * math.pi * ((((n + owner) % A * KZ + k) * (n * NZL + z)) % NZ) / NZ for n in range(A)
        ]
        return own([math.cos(x) for x in v]), own([math.sin(x) for x in v])

    def build_table():
        loads[1].wait()
        loads[2].wait()
        for z in range(NZL):
            for owner in range(A):
                for j, k in enumerate(slots):
                    cos, sin = angles(z, owner, k)
                    span = slice((j % HALF) * Q, (j % HALF + 1) * Q)
                    if owner == 0:
                        block = ed[0] * cos + ed[1] * sin
                        rows = slice(z % ZC * YL, (z % ZC + 1) * YL)
                        tf[j // HALF, z // ZC, rows, span] = block.astype(bf16)
                    block = et[0] * cos + et[1] * sin
                    tb[2 * owner + j // HALF, span, z * YL : (z + 1) * YL] = block.astype(bf16)

    spread = jnp.where(
        lax.broadcasted_iota(jnp.int32, (C * XL, C), 0) // XL
        == lax.broadcasted_iota(jnp.int32, (C * XL, C), 1),
        1.0,
        0.0,
    )

    def tall(values):
        return jnp.sum(spread * values, axis=1, keepdims=True)

    def build_lift():
        for n in (6, 7):
            loads[n].wait()
        row = lax.broadcasted_iota(jnp.int32, (C * XL, 16 * XL), 0)
        lane = lax.broadcasted_iota(jnp.int32, (C * XL, 16 * XL), 1)
        group = lane // XL
        table = jnp.zeros((C * XL, 16 * XL), f32)
        for f in range(6):
            values = tall(lw[f : f + 1, :] if f < 5 else lb[...])
            high = values.astype(bf16).astype(f32)
            rest = values - high
            if f < 5:
                table = jnp.where((group == f) | (group == 5 + f), high, table)
                table = jnp.where(group == 10 + f, rest, table)
        same = lax.rem(row, XL) == lax.rem(lane, XL)
        table = jnp.where(same & (group < 15), table, 0.0)
        table = jnp.where(lane == 15 * XL, high, table)
        table = jnp.where(lane == 15 * XL + 1, rest, table)
        wide_lift[...] = table.astype(bf16)

    with mark("ld0"):
        first.wait()
    eye = lax.broadcasted_iota(jnp.int32, (NZL * NX, NZL * NX), 0) == lax.broadcasted_iota(
        jnp.int32, (NZL * NX, NZL * NX), 1
    )
    for t in range(STEPS):
        now = state.at[t]
        for side, edge in enumerate((NY - 1, 0)):
            for f in range(5):
                column = now[f, 1 : NZL + 1, :, edge : edge + 1].reshape(NZL * NX, 1)
                ys[t, side, f : f + 1, :] = jnp.sum(
                    jnp.where(eye, jnp.broadcast_to(column, eye.shape), 0.0),
                    axis=0,
                    keepdims=True,
                )
        if t == 0:
            with mark("barrier"):
                pl.semaphore_wait(barrier, (G - 1) + (H - 1) + 1)
        for side in range(2):
            ty = lax.rem(gy + H + (1 if side == 0 else -1), H)
            remote(ys.at[t, side], yr.at[t, side], sent.at[0], hr.at[t, 0], "gy", ty).start()
        for side, edge in enumerate((NX - 1, 0)):
            for f in range(5):
                for z in range(NZL):
                    row = now[f, z + 1, edge : edge + 1, :]
                    xs[t, side, f, z : z + 1, :] = row.astype(bf16)
        for turn_of in range(2):
            side = lax.rem(gx + 1 + turn_of, 2)
            tx = lax.rem(gx + G + 1 - 2 * side, G)
            remote(xs.at[t, side], xr.at[t, side], sent.at[1], hr.at[t, 1], "gx", tx).start()
        for plane, halo in ((NZL, 0), (1, NZL + 1)):
            remote(now.at[:, plane], now.at[:, halo], sent.at[2], hr.at[t, 2], "ga", other).start()
        if t == 0:
            for load in loads:
                load.start()
            with mark("table"):
                build_table()
                loads[0].wait()
        if t == STEPS - 1:
            with mark("buildlift"):
                build_lift()
        with mark("halo%d" % t):
            remote(ys.at[t], yr.at[t], sent.at[0], hr.at[t, 0], "gy", gy).wait_recv()
            remote(xs.at[t], xr.at[t], sent.at[1], hr.at[t, 1], "gx", gx).wait_recv()
            two = now.at[:, pl.ds(0, 2)]
            remote(two, two, sent.at[2], hr.at[t, 2], "ga", other).wait_recv()
        with mark("stencil%d" % t):
            stencil_step(now, state.at[t + 1], stiff, xr.at[t], yr.at[t], (NZL, NX, NY))

    with mark("filter"):
        twin = lax.rem(lax.broadcasted_iota(jnp.int32, (2 * NY, YL), 0), NY) // 2
        twin = jnp.where(twin == lax.broadcasted_iota(jnp.int32, (2 * NY, YL), 1), 1.0, 0.0)
        for f in range(5):
            v = state[STEPS, f, 1 : NZL + 1].reshape(NZL * NX, NY)
            high = v.astype(bf16)
            rows = pl.ds(f * NZL * NX, NZL * NX)
            pairs[rows, :NY] = high
            pairs[rows, NY:] = (v - high.astype(f32)).astype(bf16)
        for rows in (pl.ds(0, 5 * NZL * XL), pl.ds(5 * NZL * XL, 5 * NZL * XL)):
            filt[rows] = dot(pairs[rows], twin.astype(bf16))

        def mean(f, z):
            start = (f * NZL + z) * NX
            both_rows = filt[pl.ds(start, XL, stride=2), :] + filt[pl.ds(start + 1, XL, stride=2), :]
            return both_rows * (0.25 * courant_half**STEPS)

        for z in range(NZL):
            v = jnp.concatenate([mean(f, z) for f in range(5)], axis=0)
            high = v.astype(bf16).astype(f32)
            v = jnp.concatenate([high, v - high, high, jnp.ones((XL, YL), f32)], axis=0)
            span = slice(z % ZC * YL, (z % ZC + 1) * YL)
            spread_in[z // ZC, :, span] = v.astype(bf16)

    with mark("lift"):
        for n in range(0, NZC, 2):
            for i in range(n, n + 2):
                lift[i] = gelu(dot(wide_lift[...], spread_in[i])).astype(bf16)
            for i in range(n, n + 2):
                remote(lift.at[i], lift_in.at[i], sent.at[3], r1s.at[i], "ga", other).start()
    for n in range(NZC):
        with mark("w1"):
            remote(lift.at[n], lift_in.at[n], sent.at[3], r1s.at[n], "ga", other).wait_recv()
        with mark("sumdiff"):
            mine, theirs = lift[n], lift_in[n]
            both[0, n] = mine + theirs
            both[1, n] = mine - theirs

    with mark("dot1"):
        for parity in range(2):
            modes = dot(both[parity, 0], tf[parity, 0])
            for n in range(1, NZC):
                modes = modes + dot(both[parity, n], tf[parity, n])
            modes = modes.astype(bf16)
            for i in range(HALF):
                p2[parity * HALF + i] = modes[:, i * Q : (i + 1) * Q].reshape(p2.shape[1:])
    for h in range(KZ):
        for peer in gx_peers:
            remote(p2.at[h, peer], r2.at[h, gx], sent.at[4], r2s.at[h], "gx", peer).start()
    for h in range(KZ):
        r2[h, gx] = p2[h, gx]

    with mark("direct"):
        loads[8].wait()
        loads[9].wait()
        bias = tall(bias_row[...])
        wide = dot(spread.astype(bf16), mix[...], ((1,), (1,))).astype(bf16)
        wide = dot(wide, spread.astype(bf16), ((1,), (1,)))
        same = lax.rem(lax.broadcasted_iota(jnp.int32, wide.shape, 0), XL) == lax.rem(
            lax.broadcasted_iota(jnp.int32, wide.shape, 1), XL
        )
        mixk = jnp.where(same, wide, 0.0).astype(bf16)
        for j in range(NZC):
            span = slice(j * ZC * YL, (j + 1) * ZC * YL)
            acc[:, span] = dot(mixk, lift[j]) + bias
        loads[3].wait()
        loads[4].wait()
        loads[5].wait()

    def turn(x, v):
        rows = x.shape[0] // 2
        return (dot(x[:rows], v) + swapped(dot(x[rows:], v))).astype(bf16)

    def staggered(h, send, size):
        @pl.when(ga == 0)
        def _():
            send(h)

        if (h + 1) % size == 0:

            @pl.when(ga != 0)
            def _():
                for i in range(h + 1 - size, h + 1):
                    send(i)

    def step_x(h):
        part = r2.at[h, pl.ds(0, G - 1)]
        with mark("w2"):
            remote(part, part, sent.at[4], r2s.at[h], "gx", gx).wait_recv()
        with mark("xdot"):
            q3[h] = turn(x1, r2[h].reshape(C * XL, Q)).reshape(q3.shape[1:])
        staggered(h, send_x, KZ)

    def send_x(h):
        for peer in gy_peers:
            remote(q3.at[h, peer], r3.at[h, gy], sent.at[5], r3s.at[h], "gy", peer).start()

    def step_y(h):
        with mark("w3"):
            part = r3.at[h, pl.ds(0, H - 1)]
            remote(part, part, sent.at[5], r3s.at[h], "gy", gy).wait_recv()
        total = q3[h, gy].astype(f32)
        for peer in gy_peers:
            total = total + r3[h, peer].astype(f32)
        c4[h] = total.astype(bf16)
        for peer in gx_peers:
            remote(c4.at[h], r4.at[h, gx], sent.at[6], r4s.at[h], "gx", peer).start()
        r4[h, gx] = c4[h]

    low = lax.broadcasted_iota(jnp.int32, (CB * KB, Q), 1) < MY

    def step_mix(h):
        part = r4.at[h, pl.ds(0, G - 1)]
        with mark("w4"):
            remote(part, part, sent.at[6], r4s.at[h], "gx", gx).wait_recv()
        with mark("mix"):
            for g in range(G):
                v = r4[h, g].astype(f32)
                turned = pltpu.roll(v, MY, 1)
                rows = pl.ds(g * CB, CB)
                rr[h, :, rows, :] = jnp.where(low, v, turned).reshape(KB, CB, Q)
                ii[h, :, rows, :] = jnp.where(low, turned, v).reshape(KB, CB, Q)

            def mix_one(kx, carry):
                a = [None] * 4
                b = [None] * 4
                for c in range(C):
                    w = wv[slots[h], kx, c]
                    x = w * rr[h, kx, c : c + 1, :]
                    y = w * ii[h, kx, c : c + 1, :]
                    n = c % 4
                    a[n] = x if a[n] is None else a[n] + x
                    b[n] = y if b[n] is None else b[n] + y
                mf[h, kx] = ((a[0] + a[1]) + (a[2] + a[3])) - swapped((b[0] + b[1]) + (b[2] + b[3]))
                return carry

            for kx in range(KB):
                mix_one(kx, 0)
            r5[h, gy] = mf[h].reshape(KB * OB, Q).astype(bf16)
        staggered(h, send_mix, HALF)

    def send_mix(h):
        for peer in gy_peers:
            remote(r5.at[h, gy], r5.at[h, gy], sent.at[7], r5s.at[h], "gy", peer).start()

    def step_back(h):
        part = r5.at[h, pl.ds(0, H - 1)]
        with mark("w5"):
            remote(part, part, sent.at[7], r5s.at[h], "gy", gy).wait_recv()
        with mark("back"):
            b6[h] = turn(x2, r5[h].reshape(H * KB * OB, Q)).reshape(b6.shape[1:])
        for peer in gx_peers:
            remote(b6.at[h, peer], r6.at[h, gx], sent.at[8], r6s.at[h], "gx", peer).start()
        r6[h, gx] = b6[h, gx]

    def step_pass(h):
        part = r6.at[h, pl.ds(0, G - 1)]
        with mark("w6"):
            remote(part, part, sent.at[8], r6s.at[h], "gx", gx).wait_recv()
        remote(r6.at[h], r7.at[h], sent.at[9], r7s.at[h], "ga", other).start()

    def modes_of(ref, parity):
        parts = [ref[parity * HALF + i].reshape(C * XL, Q) for i in range(HALF)]
        return jnp.concatenate(parts, axis=1)

    def gather(ref, owner, parity):
        with mark("zdot"):
            y = modes_of(ref, parity)
            for j in range(NZC):
                span = slice(j * ZC * YL, (j + 1) * ZC * YL)
                acc[:, span] = acc[:, span] + dot(y, tb[2 * owner + parity, :, span])

    def arrived(h):
        with mark("w7"):
            remote(r6.at[h], r7.at[h], sent.at[9], r7s.at[h], "ga", other).wait_recv()

    for h in range(KZ):
        step_x(h)
    for h in range(KZ):
        step_y(h)
    for h in range(KZ):
        step_mix(h)
    for h in range(KZ):
        step_back(h)
    for h in range(HALF):
        step_pass(h)
    gather(r6, 0, 0)
    for h in range(HALF, KZ):
        step_pass(h)
    gather(r6, 0, 1)
    for h in range(HALF):
        arrived(h)
    gather(r7, 1, 0)
    for h in range(HALF, KZ):
        arrived(h)
    with mark("final"):
        last = modes_of(r7, 1)
        for j in range(NZC):
            span = slice(j * ZC * YL, (j + 1) * ZC * YL)
            done = gelu(acc[:, span] + dot(last, tb[3, :, span])).astype(bf16)
            for z in range(ZC):
                out[j * ZC + z] = done[:, z * YL : (z + 1) * YL].reshape(C, XL, YL)

    two = state.at[pl.ds(0, STEPS), :, pl.ds(0, 2)]
    for n, (axis, ref) in enumerate(
        (
            ("gy", ys),
            ("gx", xs),
            ("ga", two),
            ("ga", lift),
            ("gx", p2.at[:, pl.ds(0, G - 1)]),
            ("gy", q3.at[:, pl.ds(0, H - 1)]),
            ("gx", r4.at[:, pl.ds(0, G - 1)]),
            ("gy", r5.at[:, pl.ds(0, H - 1)]),
            ("gx", b6.at[:, pl.ds(0, G - 1)]),
            ("ga", r6),
        )
    ):
        remote(ref, ref, sent.at[n], sent.at[n], axis, lax.axis_index(axis)).wait_send()


def east_tables(G, H, XL, C):
    CB, KB, OB = C // G, MX // H, C // G
    length = G * XL
    k = np.arange(MX) - MX // 2
    ang = 2.0 * np.pi * ((k[:, None] * np.arange(length)[None, :]) % length) / length
    scale = 1.0 / math.sqrt(length)
    cos, sin = np.cos(ang) * scale, np.sin(ang) * scale
    cos[np.abs(cos) < 1e-12] = 0.0
    sin[np.abs(sin) < 1e-12] = 0.0

    def forward(t):
        t = t.reshape(H, KB, G, XL)
        full = np.einsum("hkgx,cd->hkcgdx", t, np.eye(CB))
        return full.reshape(H * CB * KB, G * CB * XL)

    def inverse(t):
        t = t.reshape(H, KB, G, XL)
        full = np.einsum("hkgx,op->goxhkp", t, np.eye(OB))
        return full.reshape(G * OB * XL, H * KB * OB)

    x1 = np.concatenate([forward(cos), forward(sin)], axis=0)
    x2 = np.concatenate([inverse(cos), -inverse(sin)], axis=0)
    return jnp.asarray(x1, bf16), jnp.asarray(x2, bf16)


def north_tables(H, YL, NZ):
    length = H * YL
    n = np.arange(MY) - MY // 2
    u = 2.0 * np.pi * ((np.arange(length)[:, None] * n[None, :]) % length) / length
    scale = 1.0 / math.sqrt(length * NZ)
    cu, su = np.cos(u) * scale, np.sin(u) * scale
    both = np.stack([np.concatenate([cu, -su], axis=1), np.concatenate([-su, -cu], axis=1)])
    both = both.reshape(2, H, YL, 2 * MY)
    return jnp.asarray(both.transpose(1, 0, 2, 3), f32), jnp.asarray(both.transpose(1, 0, 3, 2), f32)


def shards(fields, stiffness, lift_weight, lift_bias, mix_weight, spectral_weight, output_bias):
    G, H, A = (lax.axis_size(n) for n in ("gx", "gy", "ga"))
    _, NZL, NX, NY = fields.shape
    XL, YL = NX // 2, NY // 2
    C = lift_weight.shape[1]
    CB, KB, OB, KZ, Q = C // G, MX // H, C // G, MZ // A, 2 * MY
    NZ = NZL * A
    x1, x2 = east_tables(G, H, XL, C)
    ed, et = north_tables(H, YL, NZ)
    cfg = (G, H, A, C, CB, KB, OB, KZ, NZL, XL, YL)
    vmem_bytes = 67043328 - 2 * NZL * C * XL * YL
    hbm = pl.BlockSpec(memory_space=pltpu.HBM)
    NZC, HALF = DEPTH_CHUNKS, KZ // 2
    ZW = NZL // NZC * YL
    dma = pltpu.SemaphoreType.DMA
    V = pltpu.VMEM
    return pl.pallas_call(
        functools.partial(layer_kernel, cfg),
        out_shape=V((NZL, C, XL, YL), bf16),
        in_specs=[hbm] * 11,
        out_specs=pl.BlockSpec(memory_space=V),
        scratch_shapes=[
            V((STEPS + 1, 5, NZL + 2, NX, NY), f32),
            V((NZL, NX, NY), f32),
            V((STEPS, 2, 5, NZL, NY), bf16),
            V((STEPS, 2, 5, NZL, NY), bf16),
            V((STEPS, 2, 5, NZL * NX), f32),
            V((STEPS, 2, 5, NZL * NX), f32),
            V((5 * NZL * NX, 2 * NY), bf16),
            V((5 * NZL * NX, YL), f32),
            V(ed.shape[1:], f32),
            V(et.shape[1:], f32),
            V(x1.shape, bf16),
            V(x2.shape, bf16),
            V(spectral_weight.shape, f32),
            V(lift_weight.shape, f32),
            V((1, C), f32),
            V(mix_weight.shape, bf16),
            V((1, C), f32),
            V((C * XL, 16 * XL), bf16),
            V((NZC, 16 * XL, ZW), bf16),
            V((NZC, C * XL, ZW), bf16),
            V((NZC, C * XL, ZW), bf16),
            V((2, NZC, C * XL, ZW), bf16),
            V((2, NZC, ZW, HALF * Q), bf16),
            V((2 * A, HALF * Q, NZL * YL), bf16),
            V((KZ, G, CB * XL, Q), bf16),
            V((KZ, G, CB * XL, Q), bf16),
            V((KZ, H, CB * KB, Q), bf16),
            V((KZ, H, CB * KB, Q), bf16),
            V((KZ, CB * KB, Q), bf16),
            V((KZ, G, CB * KB, Q), bf16),
            V((KZ, KB, C, Q), f32),
            V((KZ, KB, C, Q), f32),
            V((KZ, KB, OB, Q), f32),
            V((KZ, H, KB * OB, Q), bf16),
            V((KZ, G, OB * XL, Q), bf16),
            V((KZ, G, OB * XL, Q), bf16),
            V((KZ, G, OB * XL, Q), bf16),
            V((C * XL, NZL * YL), f32),
            dma((11,)), dma((10,)), dma((STEPS, 3)),
            dma((NZC,)), dma((KZ,)), dma((KZ,)), dma((KZ,)), dma((KZ,)), dma((KZ,)), dma((KZ,)),
            V((8, 128), f32),
        ],
        compiler_params=pltpu.CompilerParams(collective_id=0, has_side_effects=True, vmem_limit_bytes=vmem_bytes),
    )(
        fields, stiffness, ed, et, x1, x2, spectral_weight,
        lift_weight, lift_bias[None, :], mix_weight, output_bias[None, :],
    )


def solution(mesh):
    placed = (
        P(None, "ga", "gx", "gy"),
        P("ga", "gx", "gy"),
        P(),
        P(),
        P(),
        P("ga", "gy", None, "gx", None),
        P(),
    )
    return jax.shard_map(
        shards, mesh=mesh, in_specs=placed, out_specs=P("ga", None, "gx", "gy"), check_vma=False
    )
```

```python
import math

import contextlib
import functools
import jax
import jax.numpy as jnp
import numpy as np
from jax import lax
from jax.experimental import pallas as pl
from jax.experimental.pallas import tpu as pltpu
from jax.sharding import PartitionSpec as P

STEPS = 3
MX = 32
MY = 64
MZ = 8
DEPTH_CHUNKS = 4


courant_half = 0.1
smooth_half = 0.15
mean_flow = (0.3, -0.2, 0.1)
highest = lax.Precision.HIGHEST


MESH = pl.DeviceIdType.MESH
f32 = jnp.float32
bf16 = jnp.bfloat16


def gelu(v):
    scale = math.sqrt(2.0 / math.pi)
    half = 0.5 * v
    return half + half * jnp.tanh(v * (scale + (0.044715 * scale) * (v * v)))


def swapped(v):
    sign = jnp.where(lax.broadcasted_iota(jnp.int32, v.shape, 1) < MY, 1.0, -1.0)
    return pltpu.roll(v, MY, 1) * sign


def dot(a, b, dims=((1,), (0,))):
    return lax.dot_general(a, b, (dims, ((), ())), preferred_element_type=f32)


def line_peers(axis):
    count = lax.axis_size(axis)
    me = lax.axis_index(axis)
    order = []
    for j in range(count - 1):
        down, up = count - 1 - j, j
        down = jnp.where(down <= me, down - 1, down)
        up = jnp.where(up >= me, up + 1, up)
        order.append(jnp.where(me < count // 2, down, up))
    return me, order


def square_peers(axis):
    count = lax.axis_size(axis)
    me = lax.axis_index(axis)
    if count != 4:
        return line_peers(axis)
    flip_x = me + 1 - 2 * lax.rem(me, 2)
    return me, [3 - me, 3 - flip_x, flip_x]


def remote(src, dst, send, recv, axis, peer):
    return pltpu.make_async_remote_copy(
        src_ref=src,
        dst_ref=dst,
        send_sem=send,
        recv_sem=recv,
        device_id={axis: peer},
        device_id_type=MESH,
    )


def stencil_step(state, target, stiff, xr, yr, dims):
    NZ, NX, NY = dims
    eye = lax.broadcasted_iota(jnp.int32, (NZ * NX, NZ * NX), 0) == lax.broadcasted_iota(
        jnp.int32, (NZ * NX, NZ * NX), 1
    )
    columns = [
        [
            jnp.sum(
                jnp.where(eye, jnp.broadcast_to(yr[side, f : f + 1, :], eye.shape), 0.0),
                axis=1,
                keepdims=True,
            )
            for f in range(5)
        ]
        for side in range(2)
    ]
    weights = [
        ((smooth_half + courant_half * flow) / courant_half, (smooth_half - courant_half * flow) / courant_half)
        for flow in mean_flow
    ]
    keep = (1.0 - 6.0 * smooth_half) / courant_half
    for z in range(NZ):
        near = []
        for f in range(5):
            c = state[f, z + 1]
            span = slice(z * NX, (z + 1) * NX)
            xl = shifted(c, xr[0, f, z : z + 1, :].astype(f32), 0, 1, 8)
            xu = shifted(c, xr[1, f, z : z + 1, :].astype(f32), 0, -1, 8)
            yl = shifted(c, columns[0][f][span], 1, 1, 128)
            yu = shifted(c, columns[1][f][span], 1, -1, 128)
            near.append((c, xl, xu, yl, yu, state[f, z], state[f, z + 2]))
        diverge = (
            (near[1][2] - near[1][1]) + (near[2][4] - near[2][3]) + (near[3][6] - near[3][5])
        )
        p = near[4]
        coupling = (diverge, p[2] - p[1], p[4] - p[3], p[6] - p[5], stiff[z] * diverge)
        for f in range(5):
            c, xl, xu, yl, yu, zl, zu = near[f]
            total = c if abs(keep - 1.0) < 1e-12 else keep * c
            for (low, high), lower, upper in zip(weights, (xl, yl, zl), (xu, yu, zu)):
                total = total + (low * lower + high * upper)
            target[f, z + 1] = total - coupling[f]


def shifted(c, halo, axis, step, tile):
    count = c.shape[axis] // tile
    pieces = [lax.slice_in_dim(c, i * tile, (i + 1) * tile, axis=axis) for i in range(count)]
    rolled = [pltpu.roll(piece, step % tile, axis) for piece in pieces]
    edge = 0 if step > 0 else tile - 1
    at_edge = lax.broadcasted_iota(jnp.int32, pieces[0].shape, axis) == edge
    before = [halo] + rolled[:-1] if step > 0 else rolled[1:] + [halo]
    return jnp.concatenate([jnp.where(at_edge, b, r) for b, r in zip(before, rolled)], axis=axis)


def layer_kernel(
    cfg,
    fields_hbm, stiff_hbm, ed_hbm, et_hbm, x1_hbm, x2_hbm, w_hbm, lw_hbm, lb_hbm, mix_hbm, bias_hbm,
    out,
    state, stiff, xs, xr, ys, yr, pairs, filt, ed, et, x1, x2, wv, lw, lb, mix, bias_row, wide_lift,
    spread_in, lift, lift_in, both, tf, tb, p2, r2, q3, r3, c4, r4, rr, ii, mf, r5, b6, r6, r7, acc,
    local, sent, hr, r1s, r2s, r3s, r4s, r5s, r6s, r7s, wall,
):
    G, H, A, C, CB, KB, OB, KZ, NZL, XL, YL = cfg
    Q = 2 * MY
    NX, NY = 2 * XL, 2 * YL

    def fence():
        @pl.when(lax.axis_index("ga") < 0)
        def _():
            wall[...] = jnp.zeros_like(wall)

    @contextlib.contextmanager
    def mark(name):
        fence()
        yield

    gx, gx_peers = square_peers("gx")
    gy, gy_peers = line_peers("gy")
    ga = lax.axis_index("ga")
    other = lax.rem(ga + 1, A)
    barrier = pltpu.get_barrier_semaphore()
    for axis, group in (("gx", gx_peers), ("gy", gy_peers)):
        for peer in group:
            pl.semaphore_signal(barrier, inc=1, device_id={axis: peer}, device_id_type=MESH)
    pl.semaphore_signal(barrier, inc=1, device_id={"ga": other}, device_id_type=MESH)
    loads = [
        pltpu.make_async_copy(source, target, local.at[n])
        for n, (source, target) in enumerate(
            (
                (fields_hbm, state.at[0, :, pl.ds(1, NZL)]),
                (stiff_hbm, stiff),
                (ed_hbm.at[gy], ed),
                (et_hbm.at[gy], et),
                (x1_hbm, x1),
                (x2_hbm, x2),
                (w_hbm, wv),
                (lw_hbm, lw),
                (lb_hbm, lb),
                (mix_hbm, mix),
                (bias_hbm, bias_row),
            )
        )
    ]
    first, loads = loads[0], loads[1:]
    first.start()

    HALF = KZ // 2
    NZC = DEPTH_CHUNKS
    ZC = NZL // NZC
    NZ = NZL * A
    slots = list(range(0, KZ, 2)) + list(range(1, KZ, 2))

    def own(values):
        picked = jnp.float32(values[0])
        for n in range(1, A):
            picked = jnp.where(ga == n, jnp.float32(values[n]), picked)
        return picked

    def angles(z, owner, k):
        v = [
            2.0 * math.pi * ((((n + owner) % A * KZ + k) * (n * NZL + z)) % NZ) / NZ for n in range(A)
        ]
        return own([math.cos(x) for x in v]), own([math.sin(x) for x in v])

    def build_table():
        loads[1].wait()
        loads[2].wait()
        for z in range(NZL):
            for owner in range(A):
                for j, k in enumerate(slots):
                    cos, sin = angles(z, owner, k)
                    span = slice((j % HALF) * Q, (j % HALF + 1) * Q)
                    if owner == 0:
                        block = ed[0] * cos + ed[1] * sin
                        rows = slice(z % ZC * YL, (z % ZC + 1) * YL)
                        tf[j // HALF, z // ZC, rows, span] = block.astype(bf16)
                    block = et[0] * cos + et[1] * sin
                    tb[2 * owner + j // HALF, span, z * YL : (z + 1) * YL] = block.astype(bf16)

    spread = jnp.where(
        lax.broadcasted_iota(jnp.int32, (C * XL, C), 0) // XL
        == lax.broadcasted_iota(jnp.int32, (C * XL, C), 1),
        1.0,
        0.0,
    )

    def tall(values):
        return jnp.sum(spread * values, axis=1, keepdims=True)

    def build_lift():
        for n in (6, 7):
            loads[n].wait()
        row = lax.broadcasted_iota(jnp.int32, (C * XL, 16 * XL), 0)
        lane = lax.broadcasted_iota(jnp.int32, (C * XL, 16 * XL), 1)
        group = lane // XL
        table = jnp.zeros((C * XL, 16 * XL), f32)
        for f in range(6):
            values = tall(lw[f : f + 1, :] if f < 5 else lb[...])
            high = values.astype(bf16).astype(f32)
            rest = values - high
            if f < 5:
                table = jnp.where((group == f) | (group == 5 + f), high, table)
                table = jnp.where(group == 10 + f, rest, table)
        same = lax.rem(row, XL) == lax.rem(lane, XL)
        table = jnp.where(same & (group < 15), table, 0.0)
        table = jnp.where(lane == 15 * XL, high, table)
        table = jnp.where(lane == 15 * XL + 1, rest, table)
        wide_lift[...] = table.astype(bf16)

    with mark("ld0"):
        first.wait()
    eye = lax.broadcasted_iota(jnp.int32, (NZL * NX, NZL * NX), 0) == lax.broadcasted_iota(
        jnp.int32, (NZL * NX, NZL * NX), 1
    )
    for t in range(STEPS):
        now = state.at[t]
        for side, edge in enumerate((NY - 1, 0)):
            for f in range(5):
                column = now[f, 1 : NZL + 1, :, edge : edge + 1].reshape(NZL * NX, 1)
                ys[t, side, f : f + 1, :] = jnp.sum(
                    jnp.where(eye, jnp.broadcast_to(column, eye.shape), 0.0),
                    axis=0,
                    keepdims=True,
                )
        if t == 0:
            with mark("barrier"):
                pl.semaphore_wait(barrier, (G - 1) + (H - 1) + 1)
        for side in range(2):
            ty = lax.rem(gy + H + (1 if side == 0 else -1), H)
            remote(ys.at[t, side], yr.at[t, side], sent.at[0], hr.at[t, 0], "gy", ty).start()
        for side, edge in enumerate((NX - 1, 0)):
            for f in range(5):
                for z in range(NZL):
                    row = now[f, z + 1, edge : edge + 1, :]
                    xs[t, side, f, z : z + 1, :] = row.astype(bf16)
        for turn_of in range(2):
            side = lax.rem(gx + 1 + turn_of, 2)
            tx = lax.rem(gx + G + 1 - 2 * side, G)
            remote(xs.at[t, side], xr.at[t, side], sent.at[1], hr.at[t, 1], "gx", tx).start()
        for plane, halo in ((NZL, 0), (1, NZL + 1)):
            remote(now.at[:, plane], now.at[:, halo], sent.at[2], hr.at[t, 2], "ga", other).start()
        if t == 0:
            for load in loads:
                load.start()
            with mark("table"):
                build_table()
                loads[0].wait()
        if t == STEPS - 1:
            with mark("buildlift"):
                build_lift()
        with mark("halo%d" % t):
            remote(ys.at[t], yr.at[t], sent.at[0], hr.at[t, 0], "gy", gy).wait_recv()
            remote(xs.at[t], xr.at[t], sent.at[1], hr.at[t, 1], "gx", gx).wait_recv()
            two = now.at[:, pl.ds(0, 2)]
            remote(two, two, sent.at[2], hr.at[t, 2], "ga", other).wait_recv()
        with mark("stencil%d" % t):
            stencil_step(now, state.at[t + 1], stiff, xr.at[t], yr.at[t], (NZL, NX, NY))

    with mark("filter"):
        twin = lax.rem(lax.broadcasted_iota(jnp.int32, (2 * NY, YL), 0), NY) // 2
        twin = jnp.where(twin == lax.broadcasted_iota(jnp.int32, (2 * NY, YL), 1), 1.0, 0.0)
        for f in range(5):
            v = state[STEPS, f, 1 : NZL + 1].reshape(NZL * NX, NY)
            high = v.astype(bf16)
            rows = pl.ds(f * NZL * NX, NZL * NX)
            pairs[rows, :NY] = high
            pairs[rows, NY:] = (v - high.astype(f32)).astype(bf16)
        for rows in (pl.ds(0, 5 * NZL * XL), pl.ds(5 * NZL * XL, 5 * NZL * XL)):
            filt[rows] = dot(pairs[rows], twin.astype(bf16))

        def mean(f, z):
            start = (f * NZL + z) * NX
            both_rows = filt[pl.ds(start, XL, stride=2), :] + filt[pl.ds(start + 1, XL, stride=2), :]
            return both_rows * (0.25 * courant_half**STEPS)

        for z in range(NZL):
            v = jnp.concatenate([mean(f, z) for f in range(5)], axis=0)
            high = v.astype(bf16).astype(f32)
            v = jnp.concatenate([high, v - high, high, jnp.ones((XL, YL), f32)], axis=0)
            span = slice(z % ZC * YL, (z % ZC + 1) * YL)
            spread_in[z // ZC, :, span] = v.astype(bf16)

    with mark("lift"):
        for n in range(0, NZC, 2):
            for i in range(n, n + 2):
                lift[i] = gelu(dot(wide_lift[...], spread_in[i])).astype(bf16)
            for i in range(n, n + 2):
                remote(lift.at[i], lift_in.at[i], sent.at[3], r1s.at[i], "ga", other).start()
    for n in range(NZC):
        with mark("w1"):
            remote(lift.at[n], lift_in.at[n], sent.at[3], r1s.at[n], "ga", other).wait_recv()
        with mark("sumdiff"):
            mine, theirs = lift[n], lift_in[n]
            both[0, n] = mine + theirs
            both[1, n] = mine - theirs

    with mark("dot1"):
        for parity in range(2):
            modes = dot(both[parity, 0], tf[parity, 0])
            for n in range(1, NZC):
                modes = modes + dot(both[parity, n], tf[parity, n])
            modes = modes.astype(bf16)
            for i in range(HALF):
                p2[parity * HALF + i] = modes[:, i * Q : (i + 1) * Q].reshape(p2.shape[1:])
    for h in range(KZ):
        for peer in gx_peers:
            remote(p2.at[h, peer], r2.at[h, gx], sent.at[4], r2s.at[h], "gx", peer).start()
    for h in range(KZ):
        r2[h, gx] = p2[h, gx]

    with mark("direct"):
        loads[8].wait()
        loads[9].wait()
        bias = tall(bias_row[...])
        wide = dot(spread.astype(bf16), mix[...], ((1,), (1,))).astype(bf16)
        wide = dot(wide, spread.astype(bf16), ((1,), (1,)))
        same = lax.rem(lax.broadcasted_iota(jnp.int32, wide.shape, 0), XL) == lax.rem(
            lax.broadcasted_iota(jnp.int32, wide.shape, 1), XL
        )
        mixk = jnp.where(same, wide, 0.0).astype(bf16)
        for j in range(NZC):
            span = slice(j * ZC * YL, (j + 1) * ZC * YL)
            acc[:, span] = dot(mixk, lift[j]) + bias
        loads[3].wait()
        loads[4].wait()
        loads[5].wait()

    def turn(x, v):
        rows = x.shape[0] // 2
        return (dot(x[:rows], v) + swapped(dot(x[rows:], v))).astype(bf16)

    def staggered(h, send, size):
        @pl.when(ga == 0)
        def _():
            send(h)

        if (h + 1) % size == 0:

            @pl.when(ga != 0)
            def _():
                for i in range(h + 1 - size, h + 1):
                    send(i)

    def step_x(h):
        part = r2.at[h, pl.ds(0, G - 1)]
        with mark("w2"):
            remote(part, part, sent.at[4], r2s.at[h], "gx", gx).wait_recv()
        with mark("xdot"):
            q3[h] = turn(x1, r2[h].reshape(C * XL, Q)).reshape(q3.shape[1:])
        staggered(h, send_x, KZ)

    def send_x(h):
        for peer in gy_peers:
            remote(q3.at[h, peer], r3.at[h, gy], sent.at[5], r3s.at[h], "gy", peer).start()

    def step_y(h):
        with mark("w3"):
            part = r3.at[h, pl.ds(0, H - 1)]
            remote(part, part, sent.at[5], r3s.at[h], "gy", gy).wait_recv()
        total = q3[h, gy].astype(f32)
        for peer in gy_peers:
            total = total + r3[h, peer].astype(f32)
        c4[h] = total.astype(bf16)
        for peer in gx_peers:
            remote(c4.at[h], r4.at[h, gx], sent.at[6], r4s.at[h], "gx", peer).start()
        r4[h, gx] = c4[h]

    low = lax.broadcasted_iota(jnp.int32, (CB * KB, Q), 1) < MY

    def step_mix(h):
        part = r4.at[h, pl.ds(0, G - 1)]
        with mark("w4"):
            remote(part, part, sent.at[6], r4s.at[h], "gx", gx).wait_recv()
        with mark("mix"):
            for g in range(G):
                v = r4[h, g].astype(f32)
                turned = pltpu.roll(v, MY, 1)
                rows = pl.ds(g * CB, CB)
                rr[h, :, rows, :] = jnp.where(low, v, turned).reshape(KB, CB, Q)
                ii[h, :, rows, :] = jnp.where(low, turned, v).reshape(KB, CB, Q)

            def mix_one(kx, carry):
                a = [None] * 4
                b = [None] * 4
                for c in range(C):
                    w = wv[slots[h], kx, c]
                    x = w * rr[h, kx, c : c + 1, :]
                    y = w * ii[h, kx, c : c + 1, :]
                    n = c % 4
                    a[n] = x if a[n] is None else a[n] + x
                    b[n] = y if b[n] is None else b[n] + y
                mf[h, kx] = ((a[0] + a[1]) + (a[2] + a[3])) - swapped((b[0] + b[1]) + (b[2] + b[3]))
                return carry

            for kx in range(KB):
                mix_one(kx, 0)
            r5[h, gy] = mf[h].reshape(KB * OB, Q).astype(bf16)
        staggered(h, send_mix, HALF)

    def send_mix(h):
        for peer in gy_peers:
            remote(r5.at[h, gy], r5.at[h, gy], sent.at[7], r5s.at[h], "gy", peer).start()

    def step_back(h):
        part = r5.at[h, pl.ds(0, H - 1)]
        with mark("w5"):
            remote(part, part, sent.at[7], r5s.at[h], "gy", gy).wait_recv()
        with mark("back"):
            b6[h] = turn(x2, r5[h].reshape(H * KB * OB, Q)).reshape(b6.shape[1:])
        for peer in gx_peers:
            remote(b6.at[h, peer], r6.at[h, gx], sent.at[8], r6s.at[h], "gx", peer).start()
        r6[h, gx] = b6[h, gx]

    def step_pass(h):
        part = r6.at[h, pl.ds(0, G - 1)]
        with mark("w6"):
            remote(part, part, sent.at[8], r6s.at[h], "gx", gx).wait_recv()
        remote(r6.at[h], r7.at[h], sent.at[9], r7s.at[h], "ga", other).start()

    def modes_of(ref, parity):
        parts = [ref[parity * HALF + i].reshape(C * XL, Q) for i in range(HALF)]
        return jnp.concatenate(parts, axis=1)

    def gather(ref, owner, parity):
        with mark("zdot"):
            y = modes_of(ref, parity)
            for j in range(NZC):
                span = slice(j * ZC * YL, (j + 1) * ZC * YL)
                acc[:, span] = acc[:, span] + dot(y, tb[2 * owner + parity, :, span])

    def arrived(h):
        with mark("w7"):
            remote(r6.at[h], r7.at[h], sent.at[9], r7s.at[h], "ga", other).wait_recv()

    for h in range(KZ):
        step_x(h)
    for h in range(KZ):
        step_y(h)
    for h in range(KZ):
        step_mix(h)
    for h in range(KZ):
        step_back(h)
    for h in range(HALF):
        step_pass(h)
    gather(r6, 0, 0)
    for h in range(HALF, KZ):
        step_pass(h)
    gather(r6, 0, 1)
    for h in range(HALF):
        arrived(h)
    gather(r7, 1, 0)
    for h in range(HALF, KZ):
        arrived(h)
    with mark("final"):
        last = modes_of(r7, 1)
        for j in range(NZC):
            span = slice(j * ZC * YL, (j + 1) * ZC * YL)
            done = gelu(acc[:, span] + dot(last, tb[3, :, span])).astype(bf16)
            for z in range(ZC):
                out[j * ZC + z] = done[:, z * YL : (z + 1) * YL].reshape(C, XL, YL)

    two = state.at[pl.ds(0, STEPS), :, pl.ds(0, 2)]
    for n, (axis, ref) in enumerate(
        (
            ("gy", ys),
            ("gx", xs),
            ("ga", two),
            ("ga", lift),
            ("gx", p2.at[:, pl.ds(0, G - 1)]),
            ("gy", q3.at[:, pl.ds(0, H - 1)]),
            ("gx", r4.at[:, pl.ds(0, G - 1)]),
            ("gy", r5.at[:, pl.ds(0, H - 1)]),
            ("gx", b6.at[:, pl.ds(0, G - 1)]),
            ("ga", r6),
        )
    ):
        remote(ref, ref, sent.at[n], sent.at[n], axis, lax.axis_index(axis)).wait_send()


def east_tables(G, H, XL, C):
    CB, KB, OB = C // G, MX // H, C // G
    length = G * XL
    k = np.arange(MX) - MX // 2
    ang = 2.0 * np.pi * ((k[:, None] * np.arange(length)[None, :]) % length) / length
    scale = 1.0 / math.sqrt(length)
    cos, sin = np.cos(ang) * scale, np.sin(ang) * scale
    cos[np.abs(cos) < 1e-12] = 0.0
    sin[np.abs(sin) < 1e-12] = 0.0

    def forward(t):
        t = t.reshape(H, KB, G, XL)
        full = np.einsum("hkgx,cd->hkcgdx", t, np.eye(CB))
        return full.reshape(H * CB * KB, G * CB * XL)

    def inverse(t):
        t = t.reshape(H, KB, G, XL)
        full = np.einsum("hkgx,op->goxhkp", t, np.eye(OB))
        return full.reshape(G * OB * XL, H * KB * OB)

    x1 = np.concatenate([forward(cos), forward(sin)], axis=0)
    x2 = np.concatenate([inverse(cos), -inverse(sin)], axis=0)
    return jnp.asarray(x1, bf16), jnp.asarray(x2, bf16)


def north_tables(H, YL, NZ):
    length = H * YL
    n = np.arange(MY) - MY // 2
    u = 2.0 * np.pi * ((np.arange(length)[:, None] * n[None, :]) % length) / length
    scale = 1.0 / math.sqrt(length * NZ)
    cu, su = np.cos(u) * scale, np.sin(u) * scale
    both = np.stack([np.concatenate([cu, -su], axis=1), np.concatenate([-su, -cu], axis=1)])
    both = both.reshape(2, H, YL, 2 * MY)
    return jnp.asarray(both.transpose(1, 0, 2, 3), f32), jnp.asarray(both.transpose(1, 0, 3, 2), f32)


def shards(fields, stiffness, lift_weight, lift_bias, mix_weight, spectral_weight, output_bias):
    G, H, A = (lax.axis_size(n) for n in ("gx", "gy", "ga"))
    _, NZL, NX, NY = fields.shape
    XL, YL = NX // 2, NY // 2
    C = lift_weight.shape[1]
    CB, KB, OB, KZ, Q = C // G, MX // H, C // G, MZ // A, 2 * MY
    NZ = NZL * A
    x1, x2 = east_tables(G, H, XL, C)
    ed, et = north_tables(H, YL, NZ)
    cfg = (G, H, A, C, CB, KB, OB, KZ, NZL, XL, YL)
    vmem_bytes = 67043328 - 2 * NZL * C * XL * YL
    hbm = pl.BlockSpec(memory_space=pltpu.HBM)
    NZC, HALF = DEPTH_CHUNKS, KZ // 2
    ZW = NZL // NZC * YL
    dma = pltpu.SemaphoreType.DMA
    V = pltpu.VMEM
    return pl.pallas_call(
        functools.partial(layer_kernel, cfg),
        out_shape=V((NZL, C, XL, YL), bf16),
        in_specs=[hbm] * 11,
        out_specs=pl.BlockSpec(memory_space=V),
        scratch_shapes=[
            V((STEPS + 1, 5, NZL + 2, NX, NY), f32),
            V((NZL, NX, NY), f32),
            V((STEPS, 2, 5, NZL, NY), bf16),
            V((STEPS, 2, 5, NZL, NY), bf16),
            V((STEPS, 2, 5, NZL * NX), f32),
            V((STEPS, 2, 5, NZL * NX), f32),
            V((5 * NZL * NX, 2 * NY), bf16),
            V((5 * NZL * NX, YL), f32),
            V(ed.shape[1:], f32),
            V(et.shape[1:], f32),
            V(x1.shape, bf16),
            V(x2.shape, bf16),
            V(spectral_weight.shape, f32),
            V(lift_weight.shape, f32),
            V((1, C), f32),
            V(mix_weight.shape, bf16),
            V((1, C), f32),
            V((C * XL, 16 * XL), bf16),
            V((NZC, 16 * XL, ZW), bf16),
            V((NZC, C * XL, ZW), bf16),
            V((NZC, C * XL, ZW), bf16),
            V((2, NZC, C * XL, ZW), bf16),
            V((2, NZC, ZW, HALF * Q), bf16),
            V((2 * A, HALF * Q, NZL * YL), bf16),
            V((KZ, G, CB * XL, Q), bf16),
            V((KZ, G, CB * XL, Q), bf16),
            V((KZ, H, CB * KB, Q), bf16),
            V((KZ, H, CB * KB, Q), bf16),
            V((KZ, CB * KB, Q), bf16),
            V((KZ, G, CB * KB, Q), bf16),
            V((KZ, KB, C, Q), f32),
            V((KZ, KB, C, Q), f32),
            V((KZ, KB, OB, Q), f32),
            V((KZ, H, KB * OB, Q), bf16),
            V((KZ, G, OB * XL, Q), bf16),
            V((KZ, G, OB * XL, Q), bf16),
            V((KZ, G, OB * XL, Q), bf16),
            V((C * XL, NZL * YL), f32),
            dma((11,)), dma((10,)), dma((STEPS, 3)),
            dma((NZC,)), dma((KZ,)), dma((KZ,)), dma((KZ,)), dma((KZ,)), dma((KZ,)), dma((KZ,)),
            V((8, 128), f32),
        ],
        compiler_params=pltpu.CompilerParams(collective_id=0, has_side_effects=True, vmem_limit_bytes=vmem_bytes),
    )(
        fields, stiffness, ed, et, x1, x2, spectral_weight,
        lift_weight, lift_bias[None, :], mix_weight, output_bias[None, :],
    )


def solution(mesh):
    placed = (
        P(None, "ga", "gx", "gy"),
        P("ga", "gx", "gy"),
        P(),
        P(),
        P(),
        P("ga", "gy", None, "gx", None),
        P(),
    )
    return jax.shard_map(
        shards, mesh=mesh, in_specs=placed, out_specs=P("ga", None, "gx", "gy"), check_vma=False
    )
```
